32 devices in a mesh: ep: 16 (over z, x, core), vp: 2 (over y).
Axes of the slice: x: 2, y: 2, z: 4, core: 2. Of those that a mesh axis runs over, the one named last changes fastest.
Arguments:
- prefill_tokens: bfloat16 [1024, 2048], P('ep'), may hold values from -6 to 6
- decode_tokens: bfloat16 [64, 2048], P('ep'), may hold values from -6 to 6
- request_order: int32 [64], replicated, may hold values from 0 to 63, each once
- prefill_lengths: int32 [16], P('ep'), may hold values from 1 to 256, 2048 in all
- decode_lengths: int32 [64], P('ep'), may hold values from 1 to 256, 8192 in all
- latent_cache: bfloat16 [80, 256, 576], P('ep'), may hold values from -6 to 6
- attn_gain: float32 [2048], replicated, may hold values from 0.1 to 1.9
- w_query: bfloat16 [2048, 1536], P(None, 'vp'), may hold values from -0.125 to 0.125
- w_latent: bfloat16 [2048, 576], replicated, may hold values from -0.125 to 0.125
- latent_gain: float32 [512], replicated, may hold values from 0.1 to 1.9
- key_up: bfloat16 [512, 1024], P(None, 'vp'), may hold values from -0.5 to 0.5
- value_up: bfloat16 [512, 1024], P(None, 'vp'), may hold values from -0.25 to 0.25
- w_out: bfloat16 [1024, 2048], P('vp'), may hold values from -0.1875 to 0.1875
- ffn_gain: float32 [2048], replicated, may hold values from 0.1 to 1.9
- expert_ids: int32 [1088, 6], P('ep'), may hold values from 0 to 15, all different within a row; in each aligned block of 68 rows (0 to 67, 68 to 135, ...) at most 51 rows name the same one
- expert_weights: float32 [1088, 6], P('ep'), may hold values from 0.05 to 0.45
- w_gate: bfloat16 [16, 2048, 1408], P('ep', None, 'vp'), may hold values from -0.125 to 0.125
- w_up: bfloat16 [16, 2048, 1408], P('ep', None, 'vp'), may hold values from -0.125 to 0.125
- w_down: bfloat16 [16, 1408, 2048], P('ep', 'vp'), may hold values from -0.15625 to 0.15625
- final_gain: float32 [2048], replicated, may hold values from 0.1 to 1.9
- head_weight: bfloat16 [2048, 51200], P(None, ('ep', 'vp')), may hold values from -0.375 to 0.375
Outputs:
- layer_out: bfloat16 [1088, 2048], P('ep', 'vp')
- logits: float32 [80, 51200], P(None, ('ep', 'vp'))
The draws below stay inside these ranges and needn't reach their ends.
Inputs may be any that keep to these rules, and one draw needn't show every extreme that they name: `request_order`: each decode request appears in exactly one batch slot. `prefill_lengths`: some prefill request has 256 cached positions. `decode_lengths`: some decode request has 256 cached positions. `expert_ids`: each row names 6 different experts. Among the rows of one owner no expert is named more than 51 times, and in some owner's rows one expert is named exactly 51 times.
All inputs are finite; a program needn't handle non-finite values. No bound on the sum of `prefill_lengths` or of `decode_lengths` on one device may be relied on, other than what follows from the above.
Results may differ from the reference program's by a relative error of at most 0.0086.
Values may be sent and summed in bfloat16 or wider, within the bound.
A program may use at most 128 MiB of HBM per device.

```python
import math
import jax
import jax.numpy as jnp
import numpy as np
from jax import lax

D = 2048
H = 8
NOPE = 128
ROPE = 64
VD = 128
LAT = 512
FFE = 1408
TOPK = 6
VOCAB = 51200
CTX = 256
PREFILL = 64
DECODE = 4
ROWS_DEV = 68
TOKENS = 1088
EXPERTS = 16
CAP = 51
N_EP = 16


def steps_of(own_key, shape, cuts, smallest, largest):
    level, own = 1.0, jax.random.fold_in(own_key, 6)
    for axis_at, parts in cuts:
        heights = jnp.exp(jax.random.uniform(jax.random.fold_in(own, axis_at), (parts,), jnp.float32, smallest / len(cuts), largest / len(cuts)))
        level = level * jnp.repeat(heights, shape[axis_at] // parts).reshape([-1 if axis == axis_at else 1 for axis in range(len(shape))])
    return level


def length_profile(amount, total, most, slope):
    loads = [(1 << 20) // math.isqrt(rank ** slope) + 1 for rank in range(2, amount + 1)]
    surplus, holding = total - most - (amount - 1), [1] * (amount - 1)
    while surplus > 0:
        movable = [i for i in range(amount - 1) if holding[i] < most]
        pool, remaining = sum([loads[i] for i in movable]), surplus
        for i in movable:
            more = min(most - holding[i], max(1, remaining * loads[i] // pool), surplus)
            holding[i] = holding[i] + more
            surplus = surplus - more
    return np.array([most] + holding)


def ragged(own_key, amount, total, limit, skew):
    if amount == 2:
        one = jax.random.randint(own_key, (), max(1, total - limit), min(limit, total - 1) + 1)
        return jnp.stack([one, total - one])
    sizes = jnp.asarray(length_profile(amount, total, limit, skew), jnp.int32)
    pairs = (amount - 1) // 2
    source_of, taker = sizes[1:1 + 2 * pairs:2], sizes[2:2 + 2 * pairs:2]
    slack = jnp.minimum(source_of - 1, limit - taker)
    moved = jax.random.randint(jax.random.fold_in(own_key, 1), (pairs,), 0, 1 << 20) % (slack + 1)
    sizes = sizes.at[1:1 + 2 * pairs:2].set(source_of - moved).at[2:2 + 2 * pairs:2].set(taker + moved)
    return sizes[jax.random.permutation(jax.random.fold_in(own_key, 2), amount)]


def routed_block(rng, own, number, rows, count, top, most, lean):
    order = jax.random.permutation(rng, count)
    heavy_load, common = shares(count, rows * top, most, lean, True), shares(count, rows * top, most, lean, False)
    places = jnp.arange(count)

    def named(sizes, rotation):
        used = int((sizes > 0).sum())
        fixed = max(1, used // 4)
        shifted = fixed + (places - fixed + rotation * (used - fixed)) % max(1, count - fixed)
        return jnp.zeros((count,), jnp.int32).at[order[jnp.where(places < fixed, places, shifted)]].set(jnp.asarray(sizes, jnp.int32))

    sizes = jnp.where(number % 4 == 0, named(heavy_load, number // 4), named(common, number - number // 4 - 1))
    mixed = jax.random.permutation(jax.random.fold_in(own, 3), count)
    donor, receiver = mixed[0:count // 2 * 2:2], mixed[1:count // 2 * 2:2]
    margin = jnp.minimum(sizes[donor] - 1, most - sizes[receiver]) // 2
    margin = jnp.where((donor == order[0]) | (receiver == order[0]) | (sizes[receiver] == 0), 0, jnp.maximum(margin, 0))
    shifted = jax.random.randint(jax.random.fold_in(own, 4), (count // 2,), 0, 1 << 20) % (margin + 1)
    sizes = sizes.at[donor].add(-shifted).at[receiver].add(shifted)
    items = jnp.searchsorted(jnp.cumsum(sizes), jnp.arange(rows * top), side="right").astype(jnp.int32)
    listing = items.reshape(top, rows).T
    listing = listing[jax.random.permutation(jax.random.fold_in(own, 1), rows)]
    rotation = jax.random.randint(jax.random.fold_in(own, 2), (rows, 1), 0, top)
    return jnp.take_along_axis(listing, (jnp.arange(top)[None, :] + rotation) % top, axis=1)


def shares(amount, total, reach, lean, full):
    portions = [(1 << 20) // math.isqrt(grade ** lean) + 1 for grade in range(1, amount + 1)]
    largest = reach if full else min(reach, max(-(-total // amount), total * portions[0] // sum(portions)))
    least = 1 if total - largest >= amount - 1 else 0
    counts, surplus = [largest] + [least] * (amount - 1), total - largest - least * (amount - 1)
    while surplus > 0:
        movable = [i for i in range(1, amount) if counts[i] < largest] or [i for i in range(1, amount) if counts[i] < reach]
        whole, remaining = sum([portions[i] for i in movable]), surplus
        for i in movable:
            extra = min(reach - counts[i], max(1, remaining * portions[i] // whole), surplus)
            counts[i] = counts[i] + extra
            surplus = surplus - extra
    return np.array(counts)


def scatter_about(key, dims, width, most, split=(), kind=jnp.bfloat16):
    result = jax.random.normal(key, dims, jnp.float32) * width
    if len(split) > 0:
        result = steps_of(key, dims, split, -0.22, 0.18) * result
    return jnp.clip(result, min=-most, max=most).astype(kind)


def setup_inputs(seed: int = 0) -> dict:
    key_of = jax.random.split(jax.random.key(seed), 22)
    prefill_tokens = scatter_about(key_of[0], (N_EP * PREFILL, D), 1.0, 6.0, ((0, 16),))
    decode_tokens = scatter_about(key_of[1], (N_EP * DECODE, D), 1.0, 6.0, ((0, 16),))
    request_order = jax.random.permutation(key_of[2], N_EP * DECODE).astype(jnp.int32)
    prefill_lengths = ragged(key_of[3], N_EP, N_EP * CTX // 2, CTX, 1).astype(jnp.int32)
    decode_lengths = ragged(key_of[4], N_EP * DECODE, N_EP * DECODE * CTX // 2, CTX, 1).astype(jnp.int32)
    latent_cache = scatter_about(key_of[5], (N_EP * (1 + DECODE), CTX, LAT + ROPE), 1.0, 6.0, ((0, 16),))
    attn_gain = jnp.clip(1.0 + 0.18 * jax.random.normal(key_of[6], (D,), jnp.float32), 0.1, 1.9)
    w_query = scatter_about(key_of[7], (D, H * (NOPE + ROPE)), D ** -0.5, 0.125, ((1, 2),))
    w_latent = scatter_about(key_of[8], (D, LAT + ROPE), D ** -0.5, 0.125)
    latent_gain = jnp.clip(1.0 + 0.18 * jax.random.normal(key_of[9], (LAT,), jnp.float32), 0.1, 1.9)
    key_up = scatter_about(key_of[10], (LAT, H * NOPE), NOPE ** -0.5, 0.5, ((1, 2),))
    value_up = scatter_about(key_of[11], (LAT, H * VD), LAT ** -0.5, 0.25, ((1, 2),))
    w_out = scatter_about(key_of[12], (H * VD, D), (H * VD) ** -0.5, 0.1875, ((0, 2),))
    ffn_gain = jnp.clip(1.0 + 0.18 * jax.random.normal(key_of[13], (D,), jnp.float32), 0.1, 1.9)
    expert_ids_keys = jax.random.split(jax.random.fold_in(key_of[14], 1), TOKENS // ROWS_DEV)
    expert_ids_turns = jax.random.permutation(jax.random.fold_in(key_of[14], 3), TOKENS // ROWS_DEV)
    expert_ids = jax.vmap(lambda own, number: routed_block(jax.random.fold_in(key_of[14], 2), own, number, ROWS_DEV, EXPERTS, TOPK, CAP, 2))(expert_ids_keys, expert_ids_turns).reshape((TOKENS, TOPK))
    expert_weights = jnp.clip(0.05 + 0.39999999 * jax.random.uniform(key_of[15], (TOKENS, TOPK), jnp.float32) ** steps_of(key_of[15], (TOKENS, TOPK), ((0, 16),), -0.2, 0.2), 0.05, 0.45)
    w_gate = scatter_about(key_of[16], (EXPERTS, D, FFE), D ** -0.5, 0.125, ((0, 16), (2, 2)))
    w_up = scatter_about(key_of[17], (EXPERTS, D, FFE), D ** -0.5, 0.125, ((0, 16), (2, 2)))
    w_down = scatter_about(key_of[18], (EXPERTS, FFE, D), FFE ** -0.5, 0.15625, ((0, 16), (1, 2)))
    final_gain = jnp.clip(1.0 + 0.18 * jax.random.normal(key_of[19], (D,), jnp.float32), 0.1, 1.9)
    head_weight = scatter_about(key_of[20], (D, VOCAB), (D // 9) ** -0.5, 0.375, ((1, 32),))
    return {"prefill_tokens": prefill_tokens, "decode_tokens": decode_tokens, "request_order": request_order, "prefill_lengths": prefill_lengths, "decode_lengths": decode_lengths, "latent_cache": latent_cache, "attn_gain": attn_gain, "w_query": w_query, "w_latent": w_latent, "latent_gain": latent_gain, "key_up": key_up, "value_up": value_up, "w_out": w_out, "ffn_gain": ffn_gain, "expert_ids": expert_ids, "expert_weights": expert_weights, "w_gate": w_gate, "w_up": w_up, "w_down": w_down, "final_gain": final_gain, "head_weight": head_weight}


epsilon = 1e-06
rope_base = 10000.0

def rms_norm(values, gain):
    return values * lax.rsqrt(lax.optimization_barrier(jnp.mean(values * values, axis=-1, keepdims=True)) + epsilon) * gain

def rotate(values, positions):
    half_width = values.shape[-1] // 2
    frequency = rope_base ** (-jnp.arange(half_width, dtype=jnp.float32) * 2.0 / values.shape[-1])
    angles = positions.astype(jnp.float32)[..., None] * frequency
    cosines = jnp.cos(angles)
    sines = jnp.sin(angles)
    lower_half = values[..., :half_width]
    upper_half = values[..., half_width:]
    return jnp.concatenate([lower_half * cosines - upper_half * sines, lower_half * sines + upper_half * cosines], axis=-1)

def attend(prefill_rows, decode_rows, cached, prefill_len, decode_len, attn_gain, w_query, w_latent, latent_gain, key_up, value_up, w_out):
    tokens = jnp.concatenate([prefill_rows, decode_rows], axis=0)
    prefill_count = prefill_rows.shape[0]
    row_count = tokens.shape[0]
    head_count = w_query.shape[1] // (NOPE + ROPE)
    positions = jnp.concatenate([prefill_len[0] + jnp.arange(prefill_count, dtype=jnp.int32), decode_len.astype(jnp.int32)])
    normed = rms_norm(tokens.astype(jnp.float32), attn_gain).astype(jnp.bfloat16)
    queries = jnp.dot(normed, w_query, preferred_element_type=jnp.float32).reshape(row_count, head_count, NOPE + ROPE)
    query_nope = queries[..., :NOPE].astype(jnp.bfloat16)
    query_rope = rotate(queries[..., NOPE:], positions[:, None]).astype(jnp.bfloat16)
    latent = jnp.dot(normed, w_latent, preferred_element_type=jnp.float32)
    latent_normed = rms_norm(latent[:, :LAT], latent_gain)
    new_keys = jnp.concatenate([latent_normed, rotate(latent[:, LAT:], positions)], axis=1).astype(jnp.bfloat16)
    key_heads = key_up.reshape(LAT, head_count, NOPE)
    absorbed = jnp.einsum('rhn,lhn->rhl', query_nope.astype(jnp.float32), key_heads.astype(jnp.float32)).astype(jnp.bfloat16)
    query_all = jnp.concatenate([absorbed, query_rope], axis=-1).astype(jnp.float32)
    factor = 1.0 / jnp.sqrt(jnp.float32(NOPE + ROPE))
    cache_len = cached.shape[1]
    prefill_keys = jnp.concatenate([cached[0], new_keys[:prefill_count]], axis=0).astype(jnp.float32)
    scores = jnp.einsum('chk,jk->chj', query_all[:prefill_count], prefill_keys) * factor
    key_index = jnp.arange(cache_len + prefill_count, dtype=jnp.int32)
    row_index = jnp.arange(prefill_count, dtype=jnp.int32)
    visible = jnp.where(key_index[None, :] < cache_len, key_index[None, :] < prefill_len[0], key_index[None, :] - cache_len <= row_index[:, None])
    expo = jnp.exp(jnp.where(visible[:, None, :], scores, -jnp.inf))
    attn_probs = (expo / lax.optimization_barrier(jnp.sum(expo, axis=-1, keepdims=True))).astype(jnp.bfloat16)
    prefill_context = jnp.einsum('chj,jl->chl', attn_probs.astype(jnp.float32), prefill_keys[:, :LAT]).astype(jnp.bfloat16)
    decode_query = query_all[prefill_count:]
    decode_cache = cached[1:].astype(jnp.float32)
    own_keys = new_keys[prefill_count:].astype(jnp.float32)
    cache_scores = jnp.einsum('dhk,dsk->dhs', decode_query, decode_cache) * factor
    self_scores = jnp.einsum('dhk,dk->dh', decode_query, own_keys) * factor
    cache_visible = jnp.arange(cache_len, dtype=jnp.int32)[None, :] < decode_len[:, None]
    cache_expo = jnp.exp(jnp.where(cache_visible[:, None, :], cache_scores, -jnp.inf))
    self_expo = jnp.exp(self_scores)
    totals = lax.optimization_barrier(jnp.sum(cache_expo, axis=-1)) + self_expo
    cache_probs = (cache_expo / totals[..., None]).astype(jnp.bfloat16)
    self_probs = (self_expo / totals).astype(jnp.bfloat16)
    decode_context = jnp.einsum('dhs,dsl->dhl', cache_probs.astype(jnp.float32), decode_cache[..., :LAT])
    decode_context = (decode_context + self_probs.astype(jnp.float32)[..., None] * own_keys[:, None, :LAT]).astype(jnp.bfloat16)
    context = jnp.concatenate([prefill_context, decode_context], axis=0)
    value_heads = value_up.reshape(LAT, head_count, VD)
    head_out = jnp.einsum('rhl,lhv->rhv', context.astype(jnp.float32), value_heads.astype(jnp.float32)).astype(jnp.bfloat16)
    return jnp.dot(head_out.reshape(row_count, head_count * VD), w_out, preferred_element_type=jnp.float32)

def reference(prefill_tokens, decode_tokens, request_order, prefill_lengths, decode_lengths, latent_cache, attn_gain, w_query, w_latent, latent_gain, key_up, value_up, w_out, ffn_gain, expert_ids, expert_weights, w_gate, w_up, w_down, final_gain, head_weight):
    prefill_blocks = prefill_tokens.reshape(N_EP, PREFILL, D)
    decode_blocks = decode_tokens.reshape(N_EP, DECODE, D)
    cache_blocks = latent_cache.reshape(N_EP, 1 + DECODE, CTX, LAT + ROPE)
    prefill_len_blocks = prefill_lengths.reshape(N_EP, 1)
    decode_len_blocks = decode_lengths.reshape(N_EP, DECODE)

    def per_owner(pieces):
        return attend(pieces[0], pieces[1], pieces[2], pieces[3], pieces[4], attn_gain, w_query, w_latent, latent_gain, key_up, value_up, w_out)
    attn = lax.map(per_owner, (prefill_blocks, decode_blocks, cache_blocks, prefill_len_blocks, decode_len_blocks))
    tokens = jnp.concatenate([prefill_blocks, decode_blocks], axis=1).reshape(TOKENS, D)
    resid = (tokens.astype(jnp.float32) + attn.reshape(TOKENS, D)).astype(jnp.bfloat16)
    ffn_in = rms_norm(resid.astype(jnp.float32), ffn_gain).astype(jnp.bfloat16)
    flat_ids = expert_ids.reshape(-1)
    flat_weights = expert_weights.reshape(-1)
    assignments = TOKENS * TOPK
    room = N_EP * CAP

    def one_expert(carry, expert_index):
        picks = jnp.nonzero(flat_ids == expert_index, size=room, fill_value=assignments)[0].astype(jnp.int32)
        valid = picks < assignments
        token_rows = jnp.minimum(picks // TOPK, TOKENS - 1)
        weight = jnp.where(valid, flat_weights[jnp.minimum(picks, assignments - 1)], 0.0)
        inputs = ffn_in[token_rows]
        gated = jnp.dot(inputs, w_gate[expert_index], preferred_element_type=jnp.float32)
        upward = jnp.dot(inputs, w_up[expert_index], preferred_element_type=jnp.float32)
        hidden_act = (jax.nn.silu(gated) * upward).astype(jnp.bfloat16)
        expert_out = jnp.dot(hidden_act, w_down[expert_index], preferred_element_type=jnp.float32)
        return (carry.at[token_rows].add(weight[:, None] * expert_out), None)
    routed, _ = lax.scan(one_expert, jnp.zeros((TOKENS, D), jnp.float32), jnp.arange(EXPERTS, dtype=jnp.int32))
    layer_out = (resid.astype(jnp.float32) + routed).astype(jnp.bfloat16)
    out_blocks = layer_out.reshape(N_EP, PREFILL + DECODE, D)
    prefill_last = out_blocks[:, PREFILL - 1]
    decode_rows = out_blocks[:, PREFILL:].reshape(N_EP * DECODE, D)[request_order]
    final_rows = jnp.concatenate([prefill_last, decode_rows], axis=0)
    final_normed = rms_norm(final_rows.astype(jnp.float32), final_gain).astype(jnp.bfloat16)
    logits = jnp.dot(final_normed, head_weight, preferred_element_type=jnp.float32)
    return (layer_out, logits)
```

```python
import functools

import jax
import jax.numpy as jnp
from jax import lax
from jax.experimental import pallas as pl
from jax.experimental.pallas import tpu as pltpu
from jax.sharding import PartitionSpec as P

NOPE = 128
ROPE = 64
VD = 128
LAT = 512
TOPK = 6


epsilon = 1e-06
rope_base = 10000.0


def rms_norm(values, gain):
    return values * lax.rsqrt(jnp.mean(values * values, axis=-1, keepdims=True) + epsilon) * gain


def rotate(values, positions):
    half_width = values.shape[-1] // 2
    frequency = rope_base ** (-jnp.arange(half_width, dtype=jnp.float32) * 2.0 / values.shape[-1])
    angles = positions.astype(jnp.float32)[..., None] * frequency
    cosines = jnp.cos(angles)
    sines = jnp.sin(angles)
    lower_half = values[..., :half_width]
    upper_half = values[..., half_width:]
    return jnp.concatenate(
        [lower_half * cosines - upper_half * sines, lower_half * sines + upper_half * cosines],
        axis=-1,
    )


def attend(
    prefill_rows,
    decode_rows,
    cached,
    prefill_len,
    decode_len,
    attn_gain,
    w_query,
    w_latent,
    latent_gain,
    key_up,
    value_up,
    w_out,
):
    tokens = jnp.concatenate([prefill_rows, decode_rows], axis=0)
    prefill_count = prefill_rows.shape[0]
    row_count = tokens.shape[0]
    head_count = w_query.shape[1] // (NOPE + ROPE)
    positions = jnp.concatenate(
        [prefill_len[0] + jnp.arange(prefill_count, dtype=jnp.int32), decode_len]
    )
    normed = rms_norm(tokens.astype(jnp.float32), attn_gain).astype(jnp.bfloat16)
    queries = jnp.dot(normed, w_query, preferred_element_type=jnp.float32).reshape(
        row_count, head_count, NOPE + ROPE
    )
    query_nope = queries[..., :NOPE].astype(jnp.bfloat16)
    query_rope = rotate(queries[..., NOPE:], positions[:, None]).astype(jnp.bfloat16)
    latent = jnp.dot(normed, w_latent, preferred_element_type=jnp.float32)
    latent_normed = rms_norm(latent[:, :LAT], latent_gain)
    new_keys = jnp.concatenate([latent_normed, rotate(latent[:, LAT:], positions)], axis=1).astype(
        jnp.bfloat16
    )
    key_heads = key_up.reshape(LAT, head_count, NOPE)
    absorbed = jnp.einsum(
        "rhn,lhn->rhl", query_nope, key_heads, preferred_element_type=jnp.float32
    ).astype(jnp.bfloat16)
    query_all = jnp.concatenate([absorbed, query_rope], axis=-1)
    factor = 1.0 / jnp.sqrt(jnp.float32(NOPE + ROPE))
    cache_len = cached.shape[1]
    prefill_keys = jnp.concatenate([cached[0], new_keys[:prefill_count]], axis=0)
    scores = (
        jnp.einsum(
            "chk,jk->chj",
            query_all[:prefill_count],
            prefill_keys,
            preferred_element_type=jnp.float32,
        )
        * factor
    )
    key_index = jnp.arange(cache_len + prefill_count, dtype=jnp.int32)
    row_index = jnp.arange(prefill_count, dtype=jnp.int32)
    visible = jnp.where(
        key_index[None, :] < cache_len,
        key_index[None, :] < prefill_len[0],
        key_index[None, :] - cache_len <= row_index[:, None],
    )
    expo = jnp.exp(jnp.where(visible[:, None, :], scores, -jnp.inf))
    attn_probs = (expo / jnp.sum(expo, axis=-1, keepdims=True)).astype(jnp.bfloat16)
    prefill_context = jnp.einsum(
        "chj,jl->chl", attn_probs, prefill_keys[:, :LAT], preferred_element_type=jnp.float32
    ).astype(jnp.bfloat16)
    decode_query = query_all[prefill_count:]
    decode_cache = cached[1:]
    own_keys = new_keys[prefill_count:]
    cache_scores = (
        jnp.einsum("dhk,dsk->dhs", decode_query, decode_cache, preferred_element_type=jnp.float32)
        * factor
    )
    self_scores = (
        jnp.einsum("dhk,dk->dh", decode_query, own_keys, preferred_element_type=jnp.float32)
        * factor
    )
    cache_visible = jnp.arange(cache_len, dtype=jnp.int32)[None, :] < decode_len[:, None]
    cache_expo = jnp.exp(jnp.where(cache_visible[:, None, :], cache_scores, -jnp.inf))
    self_expo = jnp.exp(self_scores)
    totals = jnp.sum(cache_expo, axis=-1) + self_expo
    cache_probs = (cache_expo / totals[..., None]).astype(jnp.bfloat16)
    self_probs = (self_expo / totals).astype(jnp.bfloat16)
    decode_context = jnp.einsum(
        "dhs,dsl->dhl", cache_probs, decode_cache[..., :LAT], preferred_element_type=jnp.float32
    )
    decode_context = (
        decode_context
        + self_probs.astype(jnp.float32)[..., None] * own_keys[:, None, :LAT].astype(jnp.float32)
    ).astype(jnp.bfloat16)
    context = jnp.concatenate([prefill_context, decode_context], axis=0)
    value_heads = value_up.reshape(LAT, head_count, VD)
    head_out = jnp.einsum(
        "rhl,lhv->rhv", context, value_heads, preferred_element_type=jnp.float32
    ).astype(jnp.bfloat16)
    return jnp.dot(
        head_out.reshape(row_count, head_count * VD), w_out, preferred_element_type=jnp.float32
    )


MESH = pl.DeviceIdType.MESH
SLAB = 80
CODE_ROW = 72
LANES = 128
FINAL = 8


def place():
    e = lax.axis_index("ep")
    return e // 4, (e // 2) % 2, e % 2, lax.axis_index("vp")


def at(z, x, c, y):
    return {"ep": z * 4 + x * 2 + c, "vp": y}


def remote(src, dst, send, recv, target):
    return pltpu.make_async_remote_copy(
        src_ref=src, dst_ref=dst, send_sem=send, recv_sem=recv, device_id=target, device_id_type=MESH
    )


def gather_kernel(nz, part_ref, tok_ref, gain_ref, code_ref, resid_ref, all_ref, got, ys, yr, us, ur, ds, dr, xs, xr, cs, cr):
    z, x, c, y = place()
    barrier = pltpu.get_barrier_semaphore()
    for target in (at(z, x, c, 1 - y), at(z, 1 - x, c, y), at(z, x, 1 - c, y)):
        pl.semaphore_signal(barrier, inc=1, device_id=target, device_id_type=MESH)

    for k in range(1, nz):
        pl.semaphore_signal(barrier, inc=1, device_id=at((z + k) % nz, x, c, y), device_id_type=MESH)
    pl.semaphore_wait(barrier, nz + 2)

    swap = remote(part_ref, got, ys, yr, at(z, x, c, 1 - y))
    swap.start()
    swap.wait()
    mine = z * 4 + x * 2 + c
    attn = part_ref[...].astype(jnp.float32) + got[...].astype(jnp.float32)
    resid = (tok_ref[...].astype(jnp.float32) + attn).astype(jnp.bfloat16)
    resid_ref[...] = resid
    ffn_in = rms_norm(resid.astype(jnp.float32), gain_ref[...])
    all_ref[mine] = (ffn_in + code_ref[...].astype(jnp.float32)).astype(jnp.bfloat16)

    def slab(zo, xo, co):
        return all_ref.at[zo * 4 + xo * 2 + co]

    def up(step):
        s = slab(z - step, x, c)
        return remote(s, s, us.at[step], ur.at[step], at(z + 1, x, c, y))

    def up_in(step):
        s = slab(z - 1 - step, x, c)
        return remote(s, s, us.at[step], ur.at[step], at(z - 1, x, c, y))

    def down(step):
        s = slab(z + step, x, c)
        return remote(s, s, ds.at[step], dr.at[step], at(z - 1, x, c, y))

    def down_in(step):
        s = slab(z + 1 + step, x, c)
        return remote(s, s, ds.at[step], dr.at[step], at(z + 1, x, c, y))

    def across(zo):
        s = slab(zo, x, c)
        return remote(s, s, xs.at[zo], xr.at[zo], at(z, 1 - x, c, y))

    def across_in(zo):
        s = slab(zo, 1 - x, c)
        return remote(s, s, xs.at[zo], xr.at[zo], at(z, 1 - x, c, y))

    def over(zo, xo):
        s = slab(zo, xo, c)
        return remote(s, s, cs.at[xo, zo], cr.at[xo, zo], at(z, x, 1 - c, y))

    def over_in(zo, xo):
        s = slab(zo, xo, 1 - c)
        return remote(s, s, cs.at[xo, zo], cr.at[xo, zo], at(z, x, 1 - c, y))

    def when(cond, fun):
        pl.when(cond)(fun)

    when(z + 1 < nz, lambda: up(0).start())
    when(z > 0, lambda: down(0).start())
    across(z).start()
    over(z, x).start()
    for step in range(nz - 1):

        @pl.when(z - 1 - step >= 0)
        def _():
            up_in(step).wait_recv()
            if step + 1 < nz - 1:
                when(z + 1 < nz, lambda: up(step + 1).start())
            across(z - 1 - step).start()
            over(z - 1 - step, x).start()

        @pl.when(z + 1 + step < nz)
        def _():
            down_in(step).wait_recv()
            if step + 1 < nz - 1:
                when(z > 0, lambda: down(step + 1).start())
            across(z + 1 + step).start()
            over(z + 1 + step, x).start()

    def land(zo):
        across_in(zo).wait_recv()
        over(zo, 1 - x).start()

    land(z)
    for step in range(nz - 1):
        when(z - 1 - step >= 0, lambda: land(z - 1 - step))
        when(z + 1 + step < nz, lambda: land(z + 1 + step))
    for zo in range(nz):
        for xo in range(2):
            over_in(zo, xo).wait_recv()
    for zo in range(nz):
        across(zo).wait_send()
        for xo in range(2):
            over(zo, xo).wait_send()
    for step in range(nz - 1):
        when((z + 1 < nz) & (z - step >= 0), lambda: up(step).wait_send())
        when((z > 0) & (z + step < nz), lambda: down(step).wait_send())


def gather(nz, partial, tokens, gain, code):
    rows, width = tokens.shape
    dma = pltpu.SemaphoreType.DMA
    return pl.pallas_call(
        functools.partial(gather_kernel, nz),
        name="gather_tokens",
        out_shape=(
            jax.ShapeDtypeStruct((rows, width), jnp.bfloat16),
            jax.ShapeDtypeStruct((nz * 4, rows, width), jnp.bfloat16),
        ),
        in_specs=[pl.BlockSpec(memory_space=pltpu.VMEM)] * 4,
        out_specs=(pl.BlockSpec(memory_space=pltpu.VMEM),) * 2,
        scratch_shapes=[
            pltpu.VMEM((rows, width), jnp.bfloat16),
            dma,
            dma,
            dma((nz - 1,)),
            dma((nz - 1,)),
            dma((nz - 1,)),
            dma((nz - 1,)),
            dma((nz,)),
            dma((nz,)),
            dma((2, nz)),
            dma((2, nz)),
        ],
        compiler_params=pltpu.CompilerParams(
            collective_id=0, has_side_effects=True, vmem_limit_bytes=40 * 1024 * 1024
        ),
    )(partial, tokens, gain, code)


def reduce_kernel(nz, p_ref, resid_ref, out_ref, fin_ref, cin, s1, ya, xb, xa, yb, s2a, s2b, s3, zin, fbuf, c_s, c_r, ya_s, ya_r, xb_s, xb_r, xa_s, xa_r, yb_s, yb_r, z_s, z_r, f_s, f_r, g_s, g_r):
    z, x, c, y = place()
    share = s3.shape[-1]
    half = share // 2
    barrier = pltpu.get_barrier_semaphore()
    plane = [(dx, dc, dy) for dx in range(2) for dc in range(2) for dy in range(2) if (dx, dc, dy) != (0, 0, 0)]

    def beside(k):
        dx, dc, dy = plane[k]
        return at(z, (x + dx) % 2, (c + dc) % 2, (y + dy) % 2)

    def along(k):
        return at((z + k) % nz, x, c, y)

    for k in range(len(plane)):
        pl.semaphore_signal(barrier, inc=1, device_id=beside(k), device_id_type=MESH)
    for k in range(1, nz):
        pl.semaphore_signal(barrier, inc=1, device_id=along(k), device_id_type=MESH)
    pl.semaphore_wait(barrier, len(plane) + nz - 1)

    def add(a, b):
        return (a.astype(jnp.float32) + b.astype(jnp.float32)).astype(jnp.bfloat16)

    def cols(yo, part):
        return pl.ds(pl.multiple_of(yo * share + part * half, LANES), half)

    def core_copy(zo, xo):
        return remote(
            p_ref.at[zo * 4 + xo * 2 + 1 - c], cin.at[zo * 2 + xo], c_s.at[zo, xo], c_r.at[zo, xo], at(z, x, 1 - c, y)
        )

    def ya_copy(zo, xo):
        return remote(
            s1.at[zo * 2 + xo, :, cols(1 - y, 0)], ya.at[zo * 2 + xo], ya_s.at[zo, xo], ya_r.at[zo, xo], at(z, x, c, 1 - y)
        )

    def xb_copy(zo, yo):
        return remote(
            s1.at[zo * 2 + 1 - x, :, cols(yo, 1)], xb.at[zo * 2 + yo], xb_s.at[zo, yo], xb_r.at[zo, yo], at(z, 1 - x, c, y)
        )

    def xa_copy(zo):
        return remote(s2a.at[zo * 2 + 1 - x], xa.at[zo], xa_s.at[zo], xa_r.at[zo], at(z, 1 - x, c, y))

    def yb_copy(zo):
        return remote(s2b.at[zo * 2 + 1 - y], yb.at[zo], yb_s.at[zo], yb_r.at[zo], at(z, x, c, 1 - y))

    def z_copy(k):
        return remote(s3.at[(z + k) % nz], zin.at[k - 1], z_s.at[k - 1], z_r.at[k - 1], along(k))

    order = [(z + 1 + i) % nz for i in range(nz)]
    for zo in order:
        for xo in range(2):
            core_copy(zo, xo).start()
    for zo in order:
        for xo in range(2):
            core_copy(zo, xo).wait_recv()
            s1[zo * 2 + xo] = add(p_ref[zo * 4 + xo * 2 + c], cin[zo * 2 + xo])
            ya_copy(zo, xo).start()
        for yo in range(2):
            xb_copy(zo, yo).start()
    for zo in order:
        for side in range(2):
            ya_copy(zo, side).wait_recv()
            s2a[zo * 2 + side] = add(s1[zo * 2 + side, :, cols(y, 0)], ya[zo * 2 + side])
            xb_copy(zo, side).wait_recv()
            s2b[zo * 2 + side] = add(s1[zo * 2 + x, :, cols(side, 1)], xb[zo * 2 + side])
        xa_copy(zo).start()
        yb_copy(zo).start()
    for i, zo in enumerate(order):
        xa_copy(zo).wait_recv()
        yb_copy(zo).wait_recv()
        s3[zo, :, :half] = add(s2a[zo * 2 + x], xa[zo])
        s3[zo, :, half:] = add(s2b[zo * 2 + y], yb[zo])
        if i < nz - 1:
            z_copy(i + 1).start()
    total = s3[z].astype(jnp.float32)
    for k in range(1, nz):
        z_copy(k).wait_recv()
        total = total + zin[k - 1].astype(jnp.float32)
    own = resid_ref[:, pl.ds(pl.multiple_of(y * share, LANES), share)].astype(jnp.float32)
    fbuf[...] = own + total
    out_ref[...] = fbuf[...].astype(jnp.bfloat16)

    def index(zo, xo, co, yo):
        return (zo * 4 + xo * 2 + co) * 2 + yo

    mine = index(z, x, c, y)
    fin_ref[mine] = fbuf[63:71, :].astype(jnp.bfloat16)

    def f_copy(k):
        return remote(fin_ref.at[mine], fin_ref.at[mine], f_s.at[k - 1], f_r.at[k - 1], along(k))

    def g_copy(k, d):
        b = index((z + d) % nz, x, c, y)
        return remote(fin_ref.at[b], fin_ref.at[b], g_s.at[k, d], g_r.at[k, d], beside(k))

    def g_in(k, d):
        dx, dc, dy = plane[k]
        b = index((z + d) % nz, (x + dx) % 2, (c + dc) % 2, (y + dy) % 2)
        return remote(fin_ref.at[b], fin_ref.at[b], g_s.at[k, d], g_r.at[k, d], beside(k))

    def f_in(k):
        b = index((z + nz - k) % nz, x, c, y)
        return remote(fin_ref.at[b], fin_ref.at[b], f_s.at[k - 1], f_r.at[k - 1], along(k))

    for k in range(1, nz):
        f_copy(k).start()
    for k in range(len(plane)):
        g_copy(k, 0).start()
    for d in range(1, nz):
        f_in(d).wait_recv()
        for k in range(len(plane)):
            g_copy(k, nz - d).start()
    for k in range(len(plane)):
        for d in range(nz):
            g_in(k, d).wait_recv()
    for k in range(len(plane)):
        for d in range(nz):
            g_copy(k, d).wait_send()
    for k in range(1, nz):
        f_copy(k).wait_send()
        z_copy(k).wait_send()
    for zo in range(nz):
        xa_copy(zo).wait_send()
        yb_copy(zo).wait_send()
        for side in range(2):
            core_copy(zo, side).wait_send()
            ya_copy(zo, side).wait_send()
            xb_copy(zo, side).wait_send()


def reduce_rows(nz, partial, resid):
    owners, rows, width = partial.shape
    share = width // 2
    half = share // 2
    dma = pltpu.SemaphoreType.DMA
    buf = lambda *shape: pltpu.VMEM(shape, jnp.bfloat16)
    return pl.pallas_call(
        functools.partial(reduce_kernel, nz),
        name="reduce_rows",
        out_shape=(
            jax.ShapeDtypeStruct((rows, share), jnp.bfloat16),
            jax.ShapeDtypeStruct((owners * 2, FINAL, share), jnp.bfloat16),
        ),
        in_specs=[pl.BlockSpec(memory_space=pltpu.VMEM)] * 2,
        out_specs=(pl.BlockSpec(memory_space=pltpu.VMEM),) * 2,
        scratch_shapes=[
            buf(nz * 2, rows, width),
            buf(nz * 2, rows, width),
            buf(nz * 2, rows, half),
            buf(nz * 2, rows, half),
            buf(nz, rows, half),
            buf(nz, rows, half),
            buf(nz * 2, rows, half),
            buf(nz * 2, rows, half),
            buf(nz, rows, share),
            buf(nz - 1, rows, share),
            pltpu.VMEM((rows, share), jnp.float32),
        ]
        + [dma((nz, 2))] * 6
        + [dma((nz,))] * 4
        + [dma((nz - 1,))] * 4
        + [dma((7, nz))] * 2,
        compiler_params=pltpu.CompilerParams(
            collective_id=1, has_side_effects=True, vmem_limit_bytes=48 * 1024 * 1024
        ),
    )(partial, resid)


def finish(final_rows, final_gain, head_weight):
    final_normed = rms_norm(final_rows.astype(jnp.float32), final_gain).astype(jnp.bfloat16)
    return jnp.dot(final_normed, head_weight, preferred_element_type=jnp.float32)


def gate_code(expert_ids, expert_weights, owners, width):
    named = expert_ids[:, :, None] == jnp.arange(owners, dtype=jnp.int32)
    dense = jnp.sum(jnp.where(named, expert_weights[:, :, None], 0.0), axis=1)
    flat = jnp.pad(dense.T, ((0, 0), (0, LANES - dense.shape[0]))).reshape(1, width)
    high = lax.reduce_precision(flat, 8, 7)
    middle = lax.reduce_precision(flat - high, 8, 7)
    low = flat - high - middle
    code = jnp.concatenate([high, middle, low], axis=0).astype(jnp.bfloat16)
    return jnp.pad(code, ((CODE_ROW, SLAB - CODE_ROW - 3), (0, 0)))


def on_block(
    prefill_tokens,
    decode_tokens,
    request_order,
    prefill_lengths,
    decode_lengths,
    latent_cache,
    attn_gain,
    w_query,
    w_latent,
    latent_gain,
    key_up,
    value_up,
    w_out,
    ffn_gain,
    expert_ids,
    expert_weights,
    w_gate,
    w_up,
    w_down,
    final_gain,
    head_weight,
):
    owners = lax.axis_size("ep")
    nz = owners // 4
    partial_attn = attend(
        prefill_tokens,
        decode_tokens,
        latent_cache,
        prefill_lengths,
        decode_lengths,
        attn_gain,
        w_query,
        w_latent,
        latent_gain,
        key_up,
        value_up,
        w_out,
    )
    tokens = jnp.concatenate([prefill_tokens, decode_tokens], axis=0)
    row_count, width = tokens.shape
    blank = ((0, SLAB - row_count), (0, 0))
    resid, arrived = gather(
        nz,
        jnp.pad(partial_attn.astype(jnp.bfloat16), blank),
        jnp.pad(tokens, blank),
        ffn_gain.reshape(1, width),
        gate_code(expert_ids, expert_weights, owners, width),
    )
    me = lax.axis_index("ep")
    codes = lax.dynamic_slice(arrived, (0, CODE_ROW, me * LANES), (owners, 3, LANES))
    gates = jnp.sum(codes.astype(jnp.float32), axis=1)[:, :SLAB].reshape(owners * SLAB, 1)
    flattened = arrived.reshape(owners * SLAB, width)
    gated = jnp.dot(flattened, w_gate[0], preferred_element_type=jnp.float32)
    upward = jnp.dot(flattened, w_up[0], preferred_element_type=jnp.float32)
    hidden_act = (jax.nn.silu(gated) * upward).astype(jnp.bfloat16)
    result = jnp.dot(hidden_act, w_down[0], preferred_element_type=jnp.float32) * gates
    partial = result.astype(jnp.bfloat16).reshape(owners, SLAB, width)
    share_rows, everyone = reduce_rows(nz, partial, resid)
    layer_out = share_rows[:row_count]
    decode_count = decode_tokens.shape[0]
    everyone = everyone.reshape(owners, 2, FINAL, width // 2)[:, :, : 1 + decode_count]
    everyone = jnp.transpose(everyone, (0, 2, 1, 3)).reshape(owners, 1 + decode_count, width)
    prefill_last = everyone[:, 0]
    decode_rows = everyone[:, 1:].reshape(owners * decode_count, width)[request_order]
    final_rows = jnp.concatenate([prefill_last, decode_rows], axis=0)
    return (layer_out, finish(final_rows, final_gain, head_weight))


def on_device(
    prefill_tokens,
    decode_tokens,
    request_order,
    prefill_lengths,
    decode_lengths,
    latent_cache,
    attn_gain,
    w_query,
    w_latent,
    latent_gain,
    key_up,
    value_up,
    w_out,
    ffn_gain,
    expert_ids,
    expert_weights,
    w_gate,
    w_up,
    w_down,
    final_gain,
    head_weight,
):
    owners = lax.axis_size("ep")
    shards = lax.axis_size("vp")
    partial_attn = attend(
        prefill_tokens,
        decode_tokens,
        latent_cache,
        prefill_lengths,
        decode_lengths,
        attn_gain,
        w_query,
        w_latent,
        latent_gain,
        key_up,
        value_up,
        w_out,
    )
    attn = lax.psum(partial_attn, "vp")
    tokens = jnp.concatenate([prefill_tokens, decode_tokens], axis=0)
    resid = (tokens.astype(jnp.float32) + attn).astype(jnp.bfloat16)
    ffn_in = rms_norm(resid.astype(jnp.float32), ffn_gain).astype(jnp.bfloat16)
    row_count = tokens.shape[0]
    model_width = tokens.shape[1]
    share_width = model_width // shards
    capacity = max(2, min(row_count, row_count * TOPK * 2 // owners))
    flat_ids = expert_ids.reshape(-1)
    onehot = (flat_ids[:, None] == jnp.arange(owners, dtype=jnp.int32)[None, :]).astype(jnp.int32)
    earlier = jnp.cumsum(onehot, axis=0) - onehot
    slot_index = jnp.sum(earlier * onehot, axis=1)
    target = flat_ids * capacity + slot_index
    source_rows = jnp.arange(row_count * TOPK, dtype=jnp.int32) // TOPK
    outgoing = (
        jnp.zeros((owners * capacity, model_width), jnp.bfloat16)
        .at[target]
        .set(ffn_in[source_rows])
    )
    outgoing = outgoing.reshape(owners, capacity, model_width)
    arrived = lax.all_to_all(outgoing, "ep", split_axis=0, concat_axis=0, tiled=True)
    item_count = arrived.shape[1]
    flattened = arrived.reshape(owners * item_count, model_width)
    gated = jnp.dot(flattened, w_gate[0], preferred_element_type=jnp.float32)
    upward = jnp.dot(flattened, w_up[0], preferred_element_type=jnp.float32)
    hidden_act = (jax.nn.silu(gated) * upward).astype(jnp.bfloat16)
    result = jnp.dot(hidden_act, w_down[0], preferred_element_type=jnp.float32).reshape(
        owners, item_count, model_width
    )
    summed = lax.psum_scatter(result, "vp", scatter_dimension=2, tiled=True)
    sent_back = lax.all_to_all(summed, "ep", split_axis=0, concat_axis=0, tiled=True)
    picked = sent_back.reshape(owners * capacity, sent_back.shape[2])[target]
    picked = picked.reshape(row_count, TOPK, sent_back.shape[2])
    routed_sum = jnp.sum(expert_weights[:, :, None] * picked, axis=1)
    column = lax.axis_index("vp") * share_width
    resid_share = lax.dynamic_slice_in_dim(resid, column, share_width, 1)
    layer_out = (resid_share.astype(jnp.float32) + routed_sum).astype(jnp.bfloat16)
    prefill_count = prefill_tokens.shape[0]
    decode_count = decode_tokens.shape[0]
    own_rows = layer_out[prefill_count - 1 :]
    everyone = lax.all_gather(own_rows, ("ep", "vp"), axis=0, tiled=True)
    everyone = everyone.reshape(owners, shards, 1 + decode_count, share_width)
    everyone = jnp.transpose(everyone, (0, 2, 1, 3)).reshape(owners, 1 + decode_count, model_width)
    prefill_last = everyone[:, 0]
    decode_rows = everyone[:, 1:].reshape(owners * decode_count, model_width)[request_order]
    final_rows = jnp.concatenate([prefill_last, decode_rows], axis=0)
    final_normed = rms_norm(final_rows.astype(jnp.float32), final_gain).astype(jnp.bfloat16)
    logits = jnp.dot(final_normed, head_weight, preferred_element_type=jnp.float32)
    return (layer_out, logits)


def solution(mesh):
    block = mesh.shape["vp"] == 2 and mesh.shape["ep"] == 16
    return jax.shard_map(
        on_block if block else on_device,
        mesh=mesh,
        in_specs=(
            P("ep", None),
            P("ep", None),
            P(),
            P("ep"),
            P("ep"),
            P("ep", None, None),
            P(),
            P(None, "vp"),
            P(),
            P(),
            P(None, "vp"),
            P(None, "vp"),
            P("vp", None),
            P(),
            P("ep", None),
            P("ep", None),
            P("ep", None, "vp"),
            P("ep", None, "vp"),
            P("ep", "vp", None),
            P(),
            P(None, ("ep", "vp")),
        ),
        out_specs=(P("ep", "vp"), P(None, ("ep", "vp"))),
        check_vma=False,
    )
```

```python
import functools

import jax
import jax.numpy as jnp
from jax import lax
from jax.experimental import pallas as pl
from jax.experimental.pallas import tpu as pltpu
from jax.sharding import PartitionSpec as P

NOPE = 128
ROPE = 64
VD = 128
LAT = 512
TOPK = 6


epsilon = 1e-06
rope_base = 10000.0


def rms_norm(values, gain):
    return values * lax.rsqrt(jnp.mean(values * values, axis=-1, keepdims=True) + epsilon) * gain


def rotate(values, positions):
    half_width = values.shape[-1] // 2
    frequency = rope_base ** (-jnp.arange(half_width, dtype=jnp.float32) * 2.0 / values.shape[-1])
    angles = positions.astype(jnp.float32)[..., None] * frequency
    cosines = jnp.cos(angles)
    sines = jnp.sin(angles)
    lower_half = values[..., :half_width]
    upper_half = values[..., half_width:]
    return jnp.concatenate(
        [lower_half * cosines - upper_half * sines, lower_half * sines + upper_half * cosines],
        axis=-1,
    )


def attend(
    prefill_rows,
    decode_rows,
    cached,
    prefill_len,
    decode_len,
    attn_gain,
    w_query,
    w_latent,
    latent_gain,
    key_up,
    value_up,
    w_out,
):
    tokens = jnp.concatenate([prefill_rows, decode_rows], axis=0)
    prefill_count = prefill_rows.shape[0]
    row_count = tokens.shape[0]
    head_count = w_query.shape[1] // (NOPE + ROPE)
    positions = jnp.concatenate(
        [prefill_len[0] + jnp.arange(prefill_count, dtype=jnp.int32), decode_len]
    )
    normed = rms_norm(tokens.astype(jnp.float32), attn_gain).astype(jnp.bfloat16)
    queries = jnp.dot(normed, w_query, preferred_element_type=jnp.float32).reshape(
        row_count, head_count, NOPE + ROPE
    )
    query_nope = queries[..., :NOPE].astype(jnp.bfloat16)
    query_rope = rotate(queries[..., NOPE:], positions[:, None]).astype(jnp.bfloat16)
    latent = jnp.dot(normed, w_latent, preferred_element_type=jnp.float32)
    latent_normed = rms_norm(latent[:, :LAT], latent_gain)
    new_keys = jnp.concatenate([latent_normed, rotate(latent[:, LAT:], positions)], axis=1).astype(
        jnp.bfloat16
    )
    key_heads = key_up.reshape(LAT, head_count, NOPE)
    absorbed = jnp.einsum(
        "rhn,lhn->rhl", query_nope, key_heads, preferred_element_type=jnp.float32
    ).astype(jnp.bfloat16)
    query_all = jnp.concatenate([absorbed, query_rope], axis=-1)
    factor = 1.0 / jnp.sqrt(jnp.float32(NOPE + ROPE))
    cache_len = cached.shape[1]
    prefill_keys = jnp.concatenate([cached[0], new_keys[:prefill_count]], axis=0)
    scores = (
        jnp.einsum(
            "chk,jk->chj",
            query_all[:prefill_count],
            prefill_keys,
            preferred_element_type=jnp.float32,
        )
        * factor
    )
    key_index = jnp.arange(cache_len + prefill_count, dtype=jnp.int32)
    row_index = jnp.arange(prefill_count, dtype=jnp.int32)
    visible = jnp.where(
        key_index[None, :] < cache_len,
        key_index[None, :] < prefill_len[0],
        key_index[None, :] - cache_len <= row_index[:, None],
    )
    expo = jnp.exp(jnp.where(visible[:, None, :], scores, -jnp.inf))
    attn_probs = (expo / jnp.sum(expo, axis=-1, keepdims=True)).astype(jnp.bfloat16)
    prefill_context = jnp.einsum(
        "chj,jl->chl", attn_probs, prefill_keys[:, :LAT], preferred_element_type=jnp.float32
    ).astype(jnp.bfloat16)
    decode_query = query_all[prefill_count:]
    decode_cache = cached[1:]
    own_keys = new_keys[prefill_count:]
    cache_scores = (
        jnp.einsum("dhk,dsk->dhs", decode_query, decode_cache, preferred_element_type=jnp.float32)
        * factor
    )
    self_scores = (
        jnp.einsum("dhk,dk->dh", decode_query, own_keys, preferred_element_type=jnp.float32)
        * factor
    )
    cache_visible = jnp.arange(cache_len, dtype=jnp.int32)[None, :] < decode_len[:, None]
    cache_expo = jnp.exp(jnp.where(cache_visible[:, None, :], cache_scores, -jnp.inf))
    self_expo = jnp.exp(self_scores)
    totals = jnp.sum(cache_expo, axis=-1) + self_expo
    cache_probs = (cache_expo / totals[..., None]).astype(jnp.bfloat16)
    self_probs = (self_expo / totals).astype(jnp.bfloat16)
    decode_context = jnp.einsum(
        "dhs,dsl->dhl", cache_probs, decode_cache[..., :LAT], preferred_element_type=jnp.float32
    )
    decode_context = (
        decode_context
        + self_probs.astype(jnp.float32)[..., None] * own_keys[:, None, :LAT].astype(jnp.float32)
    ).astype(jnp.bfloat16)
    context = jnp.concatenate([prefill_context, decode_context], axis=0)
    value_heads = value_up.reshape(LAT, head_count, VD)
    head_out = jnp.einsum(
        "rhl,lhv->rhv", context, value_heads, preferred_element_type=jnp.float32
    ).astype(jnp.bfloat16)
    return jnp.dot(
        head_out.reshape(row_count, head_count * VD), w_out, preferred_element_type=jnp.float32
    )


MESH = pl.DeviceIdType.MESH
SLAB = 80
CODE_ROW = 72
LANES = 128
FINAL = 8


def place():
    e = lax.axis_index("ep")
    return e // 4, (e // 2) % 2, e % 2, lax.axis_index("vp")


def at(z, x, c, y):
    return {"ep": z * 4 + x * 2 + c, "vp": y}


def remote(src, dst, send, recv, target):
    return pltpu.make_async_remote_copy(
        src_ref=src, dst_ref=dst, send_sem=send, recv_sem=recv, device_id=target, device_id_type=MESH
    )


def gather_kernel(nz, part_ref, tok_ref, gain_ref, code_ref, resid_ref, all_ref, got, ys, yr, us, ur, ds, dr, xs, xr, cs, cr):
    z, x, c, y = place()
    barrier = pltpu.get_barrier_semaphore()
    for target in (at(z, x, c, 1 - y), at(z, 1 - x, c, y), at(z, x, 1 - c, y)):
        pl.semaphore_signal(barrier, inc=1, device_id=target, device_id_type=MESH)

    for k in range(1, nz):
        pl.semaphore_signal(barrier, inc=1, device_id=at((z + k) % nz, x, c, y), device_id_type=MESH)
    pl.semaphore_wait(barrier, nz + 2)

    swap = remote(part_ref, got, ys, yr, at(z, x, c, 1 - y))
    swap.start()
    swap.wait()
    mine = z * 4 + x * 2 + c
    attn = part_ref[...].astype(jnp.float32) + got[...].astype(jnp.float32)
    resid = (tok_ref[...].astype(jnp.float32) + attn).astype(jnp.bfloat16)
    resid_ref[...] = resid
    ffn_in = rms_norm(resid.astype(jnp.float32), gain_ref[...])
    all_ref[mine] = (ffn_in + code_ref[...].astype(jnp.float32)).astype(jnp.bfloat16)

    def slab(zo, xo, co):
        return all_ref.at[zo * 4 + xo * 2 + co]

    def up(step):
        s = slab(z - step, x, c)
        return remote(s, s, us.at[step], ur.at[step], at(z + 1, x, c, y))

    def up_in(step):
        s = slab(z - 1 - step, x, c)
        return remote(s, s, us.at[step], ur.at[step], at(z - 1, x, c, y))

    def down(step):
        s = slab(z + step, x, c)
        return remote(s, s, ds.at[step], dr.at[step], at(z - 1, x, c, y))

    def down_in(step):
        s = slab(z + 1 + step, x, c)
        return remote(s, s, ds.at[step], dr.at[step], at(z + 1, x, c, y))

    def across(zo):
        s = slab(zo, x, c)
        return remote(s, s, xs.at[zo], xr.at[zo], at(z, 1 - x, c, y))

    def across_in(zo):
        s = slab(zo, 1 - x, c)
        return remote(s, s, xs.at[zo], xr.at[zo], at(z, 1 - x, c, y))

    def over(zo, xo):
        s = slab(zo, xo, c)
        return remote(s, s, cs.at[xo, zo], cr.at[xo, zo], at(z, x, 1 - c, y))

    def over_in(zo, xo):
        s = slab(zo, xo, 1 - c)
        return remote(s, s, cs.at[xo, zo], cr.at[xo, zo], at(z, x, 1 - c, y))

    def when(cond, fun):
        pl.when(cond)(fun)

    when(z + 1 < nz, lambda: up(0).start())
    when(z > 0, lambda: down(0).start())
    across(z).start()
    over(z, x).start()
    for step in range(nz - 1):

        @pl.when(z - 1 - step >= 0)
        def _():
            up_in(step).wait_recv()
            if step + 1 < nz - 1:
                when(z + 1 < nz, lambda: up(step + 1).start())
            across(z - 1 - step).start()
            over(z - 1 - step, x).start()

        @pl.when(z + 1 + step < nz)
        def _():
            down_in(step).wait_recv()
            if step + 1 < nz - 1:
                when(z > 0, lambda: down(step + 1).start())
            across(z + 1 + step).start()
            over(z + 1 + step, x).start()

    def land(zo):
        across_in(zo).wait_recv()
        over(zo, 1 - x).start()

    land(z)
    for step in range(nz - 1):
        when(z - 1 - step >= 0, lambda: land(z - 1 - step))
        when(z + 1 + step < nz, lambda: land(z + 1 + step))
    for zo in range(nz):
        for xo in range(2):
            over_in(zo, xo).wait_recv()
    for zo in range(nz):
        across(zo).wait_send()
        for xo in range(2):
            over(zo, xo).wait_send()
    for step in range(nz - 1):
        when((z + 1 < nz) & (z - step >= 0), lambda: up(step).wait_send())
        when((z > 0) & (z + step < nz), lambda: down(step).wait_send())


def gather(nz, partial, tokens, gain, code):
    rows, width = tokens.shape
    dma = pltpu.SemaphoreType.DMA
    return pl.pallas_call(
        functools.partial(gather_kernel, nz),
        name="gather_tokens",
        out_shape=(
            jax.ShapeDtypeStruct((rows, width), jnp.bfloat16),
            jax.ShapeDtypeStruct((nz * 4, rows, width), jnp.bfloat16),
        ),
        in_specs=[pl.BlockSpec(memory_space=pltpu.VMEM)] * 4,
        out_specs=(pl.BlockSpec(memory_space=pltpu.VMEM),) * 2,
        scratch_shapes=[
            pltpu.VMEM((rows, width), jnp.bfloat16),
            dma,
            dma,
            dma((nz - 1,)),
            dma((nz - 1,)),
            dma((nz - 1,)),
            dma((nz - 1,)),
            dma((nz,)),
            dma((nz,)),
            dma((2, nz)),
            dma((2, nz)),
        ],
        compiler_params=pltpu.CompilerParams(
            collective_id=0, has_side_effects=True, vmem_limit_bytes=40 * 1024 * 1024
        ),
    )(partial, tokens, gain, code)


def reduce_kernel(nz, p_ref, resid_ref, gain_ref, out_ref, normed_ref, fin_ref, cin, s1, ya, xb, xa, yb, s2a, s2b, s3, zin, fbuf, c_s, c_r, ya_s, ya_r, xb_s, xb_r, xa_s, xa_r, yb_s, yb_r, z_s, z_r, f_s, f_r, g_s, g_r):
    z, x, c, y = place()
    share = s3.shape[-1]
    half = share // 2
    barrier = pltpu.get_barrier_semaphore()
    plane = [(dx, dc, dy) for dx in range(2) for dc in range(2) for dy in range(2) if (dx, dc, dy) != (0, 0, 0)]

    def beside(k):
        dx, dc, dy = plane[k]
        return at(z, (x + dx) % 2, (c + dc) % 2, (y + dy) % 2)

    def along(k):
        return at((z + k) % nz, x, c, y)

    for k in range(len(plane)):
        pl.semaphore_signal(barrier, inc=1, device_id=beside(k), device_id_type=MESH)
    for k in range(1, nz):
        pl.semaphore_signal(barrier, inc=1, device_id=along(k), device_id_type=MESH)
    pl.semaphore_wait(barrier, len(plane) + nz - 1)

    def add(a, b):
        return (a.astype(jnp.float32) + b.astype(jnp.float32)).astype(jnp.bfloat16)

    def cols(yo, part):
        return pl.ds(pl.multiple_of(yo * share + part * half, LANES), half)

    def core_copy(zo, xo):
        return remote(
            p_ref.at[zo * 4 + xo * 2 + 1 - c], cin.at[zo * 2 + xo], c_s.at[zo, xo], c_r.at[zo, xo], at(z, x, 1 - c, y)
        )

    def ya_copy(zo, xo):
        return remote(
            s1.at[zo * 2 + xo, :, cols(1 - y, 0)], ya.at[zo * 2 + xo], ya_s.at[zo, xo], ya_r.at[zo, xo], at(z, x, c, 1 - y)
        )

    def xb_copy(zo, yo):
        return remote(
            s1.at[zo * 2 + 1 - x, :, cols(yo, 1)], xb.at[zo * 2 + yo], xb_s.at[zo, yo], xb_r.at[zo, yo], at(z, 1 - x, c, y)
        )

    def xa_copy(zo):
        return remote(s2a.at[zo * 2 + 1 - x], xa.at[zo], xa_s.at[zo], xa_r.at[zo], at(z, 1 - x, c, y))

    def yb_copy(zo):
        return remote(s2b.at[zo * 2 + 1 - y], yb.at[zo], yb_s.at[zo], yb_r.at[zo], at(z, x, c, 1 - y))

    def z_copy(k):
        return remote(s3.at[(z + k) % nz], zin.at[k - 1], z_s.at[k - 1], z_r.at[k - 1], along(k))

    order = [(z + 1 + i) % nz for i in range(nz)]
    for zo in order:
        for xo in range(2):
            core_copy(zo, xo).start()
    for zo in order:
        for xo in range(2):
            core_copy(zo, xo).wait_recv()
            s1[zo * 2 + xo] = add(p_ref[zo * 4 + xo * 2 + c], cin[zo * 2 + xo])
            ya_copy(zo, xo).start()
        for yo in range(2):
            xb_copy(zo, yo).start()
    for zo in order:
        for side in range(2):
            ya_copy(zo, side).wait_recv()
            s2a[zo * 2 + side] = add(s1[zo * 2 + side, :, cols(y, 0)], ya[zo * 2 + side])
            xb_copy(zo, side).wait_recv()
            s2b[zo * 2 + side] = add(s1[zo * 2 + x, :, cols(side, 1)], xb[zo * 2 + side])
        xa_copy(zo).start()
        yb_copy(zo).start()
    for i, zo in enumerate(order):
        xa_copy(zo).wait_recv()
        yb_copy(zo).wait_recv()
        s3[zo, :, :half] = add(s2a[zo * 2 + x], xa[zo])
        s3[zo, :, half:] = add(s2b[zo * 2 + y], yb[zo])
        if i < nz - 1:
            z_copy(i + 1).start()
    total = s3[z].astype(jnp.float32)
    for k in range(1, nz):
        z_copy(k).wait_recv()
        total = total + zin[k - 1].astype(jnp.float32)
    own = resid_ref[:, pl.ds(pl.multiple_of(y * share, LANES), share)].astype(jnp.float32)
    fbuf[...] = own + total
    out_ref[...] = fbuf[: out_ref.shape[0], :].astype(jnp.bfloat16)

    def piece(zo, xo, co, yo):
        return fin_ref.at[zo * 4 + xo * 2 + co, :, pl.ds(pl.multiple_of(yo * share, LANES), share)]

    mine = z * 4 + x * 2 + c
    fin_ref[mine, :, pl.ds(pl.multiple_of(y * share, LANES), share)] = fbuf[63:71, :].astype(jnp.bfloat16)

    def f_copy(k):
        b = piece(z, x, c, y)
        return remote(b, b, f_s.at[k - 1], f_r.at[k - 1], along(k))

    def g_copy(k, d):
        b = piece((z + d) % nz, x, c, y)
        return remote(b, b, g_s.at[k, d], g_r.at[k, d], beside(k))

    def g_in(k, d):
        dx, dc, dy = plane[k]
        b = piece((z + d) % nz, (x + dx) % 2, (c + dc) % 2, (y + dy) % 2)
        return remote(b, b, g_s.at[k, d], g_r.at[k, d], beside(k))

    def f_in(k):
        b = piece((z + nz - k) % nz, x, c, y)
        return remote(b, b, f_s.at[k - 1], f_r.at[k - 1], along(k))

    for k in range(1, nz):
        f_copy(k).start()
    for k in range(len(plane)):
        g_copy(k, 0).start()
    for d in range(1, nz):
        f_in(d).wait_recv()
        for k in range(len(plane)):
            g_copy(k, nz - d).start()
    for k in range(len(plane)):
        for d in range(nz):
            g_in(k, d).wait_recv()
    rows = rms_norm(fin_ref[...].astype(jnp.float32), gain_ref[...])
    normed_ref[...] = rows.reshape(normed_ref.shape).astype(jnp.bfloat16)
    for k in range(len(plane)):
        for d in range(nz):
            g_copy(k, d).wait_send()
    for k in range(1, nz):
        f_copy(k).wait_send()
        z_copy(k).wait_send()
    for zo in range(nz):
        xa_copy(zo).wait_send()
        yb_copy(zo).wait_send()
        for side in range(2):
            core_copy(zo, side).wait_send()
            ya_copy(zo, side).wait_send()
            xb_copy(zo, side).wait_send()


def reduce_rows(nz, partial, resid, gain, row_count):
    owners, rows, width = partial.shape
    share = width // 2
    half = share // 2
    dma = pltpu.SemaphoreType.DMA
    buf = lambda *shape: pltpu.VMEM(shape, jnp.bfloat16)
    return pl.pallas_call(
        functools.partial(reduce_kernel, nz),
        name="reduce_rows",
        out_shape=(
            jax.ShapeDtypeStruct((row_count, share), jnp.bfloat16),
            jax.ShapeDtypeStruct((owners * FINAL, width), jnp.bfloat16),
        ),
        in_specs=[pl.BlockSpec(memory_space=pltpu.VMEM)] * 3,
        out_specs=(pl.BlockSpec(memory_space=pltpu.VMEM),) * 2,
        scratch_shapes=[
            buf(owners, FINAL, width),
            buf(nz * 2, rows, width),
            buf(nz * 2, rows, width),
            buf(nz * 2, rows, half),
            buf(nz * 2, rows, half),
            buf(nz, rows, half),
            buf(nz, rows, half),
            buf(nz * 2, rows, half),
            buf(nz * 2, rows, half),
            buf(nz, rows, share),
            buf(nz - 1, rows, share),
            pltpu.VMEM((rows, share), jnp.float32),
        ]
        + [dma((nz, 2))] * 6
        + [dma((nz,))] * 4
        + [dma((nz - 1,))] * 4
        + [dma((7, nz))] * 2,
        compiler_params=pltpu.CompilerParams(
            collective_id=1, has_side_effects=True, vmem_limit_bytes=48 * 1024 * 1024
        ),
    )(partial, resid, gain)


def attention_kernel(heads, pf, rows_of, tok_ref, gain_ref, cos_ref, sin_ref, len_ref, lgain_ref, wq_hbm, wl_hbm, cache_hbm, ku_hbm, vu_hbm, wo_hbm, out_ref, wq, wl, cache, ku, vu, wo, sems):
    pairs = [(wq_hbm, wq), (wl_hbm, wl), (cache_hbm, cache), (ku_hbm, ku), (vu_hbm, vu), (wo_hbm, wo)]
    loads = [pltpu.make_async_copy(a, b, sems.at[i]) for i, (a, b) in enumerate(pairs)]
    for load in loads:
        load.start()
    rows = tok_ref.shape[0]
    f32, bf16 = jnp.float32, jnp.bfloat16
    dot = functools.partial(jnp.dot, preferred_element_type=f32)
    nt = lambda a, b: lax.dot_general(a, b, (((1,), (1,)), ((), ())), preferred_element_type=f32)
    normed = rms_norm(tok_ref[...].astype(f32), gain_ref[...]).astype(bf16)
    cosines, sines = cos_ref[...], sin_ref[...]

    def turn(v):
        half = ROPE // 2
        return v * cosines + jnp.concatenate([v[:, half:], v[:, :half]], axis=1) * sines

    loads[0].wait()
    queries = dot(normed, wq[...])
    loads[1].wait()
    latent = dot(normed, wl[...])
    key_lat = rms_norm(latent[:, :LAT], lgain_ref[...]).astype(bf16)
    key_rope = turn(latent[:, LAT:]).astype(bf16)
    loads[2].wait()
    entries, cache_len = cache.shape[0], cache.shape[1]
    old_lat = cache[:, :, :LAT].reshape(entries * cache_len, LAT)
    old_rope = cache[:, :, LAT:].reshape(entries * cache_len, ROPE)
    row = lax.broadcasted_iota(jnp.int32, (rows, 1), 0)
    entry = jnp.where(row < pf, 0, jnp.where(row < rows_of, row - pf + 1, entries))
    start = entry * cache_len
    key = lax.broadcasted_iota(jnp.int32, (rows, entries * cache_len), 1)
    old_seen = (key >= start) & (key < start + len_ref[...])
    col = lax.broadcasted_iota(jnp.int32, (rows, rows), 1)
    new_seen = (col == row) | ((row < pf) & (col <= row))
    factor = 1.0 / jnp.sqrt(jnp.float32(NOPE + ROPE))
    loads[3].wait()
    outs = []
    for h in range(heads):
        base = h * (NOPE + ROPE)
        q_nope = queries[:, base : base + NOPE].astype(bf16)
        q_rope = turn(queries[:, base + NOPE : base + NOPE + ROPE]).astype(bf16)
        absorbed = nt(q_nope, ku[:, h * NOPE : (h + 1) * NOPE]).astype(bf16)
        old = (nt(absorbed, old_lat) + nt(q_rope, old_rope)) * factor
        new = (nt(absorbed, key_lat) + nt(q_rope, key_rope)) * factor
        old = jnp.exp(jnp.where(old_seen, old, -jnp.inf))
        new = jnp.exp(jnp.where(new_seen, new, -jnp.inf))
        total = jnp.sum(old, axis=1, keepdims=True) + jnp.sum(new, axis=1, keepdims=True)
        old = (old / total).astype(bf16)
        new = (new / total).astype(bf16)
        context = (dot(old, old_lat) + dot(new, key_lat)).astype(bf16)
        if h == 0:
            loads[4].wait()
        outs.append(dot(context, vu[:, h * VD : (h + 1) * VD]).astype(bf16))
    loads[5].wait()
    out_ref[...] = dot(jnp.concatenate(outs, axis=1), wo[...]).astype(bf16)


def attention(tokens, pf, nd, prefill_len, decode_len, cached, attn_gain, w_query, w_latent, latent_gain, key_up, value_up, w_out):
    rows, width = tokens.shape
    spare = rows - pf - nd
    steps = jnp.arange(pf, dtype=jnp.int32)
    none = jnp.zeros((spare,), jnp.int32)
    positions = jnp.concatenate([prefill_len[0] + steps, decode_len, none])
    lengths = jnp.concatenate([prefill_len[0] + 0 * steps, decode_len, none])[:, None]
    half = ROPE // 2
    frequency = rope_base ** (-jnp.arange(half, dtype=jnp.float32) * 2.0 / ROPE)
    angles = positions.astype(jnp.float32)[:, None] * frequency
    cosines, sines = jnp.cos(angles), jnp.sin(angles)
    vmem = pl.BlockSpec(memory_space=pltpu.VMEM)
    hbm = pl.BlockSpec(memory_space=pl.ANY)
    large = (w_query, w_latent, cached, key_up, value_up, w_out)
    return pl.pallas_call(
        functools.partial(attention_kernel, w_query.shape[1] // (NOPE + ROPE), pf, pf + nd),
        name="attention",
        out_shape=jax.ShapeDtypeStruct((rows, width), jnp.bfloat16),
        in_specs=[vmem] * 6 + [hbm] * 6,
        out_specs=vmem,
        scratch_shapes=[pltpu.VMEM(a.shape, a.dtype) for a in large] + [pltpu.SemaphoreType.DMA((6,))],
        compiler_params=pltpu.CompilerParams(vmem_limit_bytes=40 * 1024 * 1024),
    )(
        tokens,
        attn_gain.reshape(1, width),
        jnp.concatenate([cosines, cosines], axis=1),
        jnp.concatenate([-sines, sines], axis=1),
        lengths,
        latent_gain.reshape(1, LAT),
        *large,
    )


def gate_code(expert_ids, expert_weights, owners, width):
    named = expert_ids[:, :, None] == jnp.arange(owners, dtype=jnp.int32)
    dense = jnp.sum(jnp.where(named, expert_weights[:, :, None], 0.0), axis=1)
    flat = jnp.pad(dense.T, ((0, 0), (0, LANES - dense.shape[0]))).reshape(1, width)
    high = lax.reduce_precision(flat, 8, 7)
    middle = lax.reduce_precision(flat - high, 8, 7)
    low = flat - high - middle
    code = jnp.concatenate([high, middle, low], axis=0).astype(jnp.bfloat16)
    return jnp.pad(code, ((CODE_ROW, SLAB - CODE_ROW - 3), (0, 0)))


def on_block(
    prefill_tokens,
    decode_tokens,
    request_order,
    prefill_lengths,
    decode_lengths,
    latent_cache,
    attn_gain,
    w_query,
    w_latent,
    latent_gain,
    key_up,
    value_up,
    w_out,
    ffn_gain,
    expert_ids,
    expert_weights,
    w_gate,
    w_up,
    w_down,
    final_gain,
    head_weight,
):
    owners = lax.axis_size("ep")
    nz = owners // 4
    tokens = jnp.concatenate([prefill_tokens, decode_tokens], axis=0)
    row_count, width = tokens.shape
    prefill_count, decode_count = prefill_tokens.shape[0], decode_tokens.shape[0]
    tokens = jnp.pad(tokens, ((0, SLAB - row_count), (0, 0)))
    partial_attn = attention(
        tokens,
        prefill_count,
        decode_count,
        prefill_lengths,
        decode_lengths,
        latent_cache,
        attn_gain,
        w_query,
        w_latent,
        latent_gain,
        key_up,
        value_up,
        w_out,
    )
    resid, arrived = gather(
        nz,
        partial_attn,
        tokens,
        ffn_gain.reshape(1, width),
        gate_code(expert_ids, expert_weights, owners, width),
    )
    me = lax.axis_index("ep")
    codes = lax.dynamic_slice(arrived, (0, CODE_ROW, me * LANES), (owners, 3, LANES))
    gates = jnp.sum(codes.astype(jnp.float32), axis=1)[:, :SLAB].reshape(owners * SLAB, 1)
    flattened = arrived.reshape(owners * SLAB, width)
    gated = jnp.dot(flattened, w_gate[0], preferred_element_type=jnp.float32)
    upward = jnp.dot(flattened, w_up[0], preferred_element_type=jnp.float32)
    hidden_act = (jax.nn.silu(gated) * upward).astype(jnp.bfloat16)
    result = jnp.dot(hidden_act, w_down[0], preferred_element_type=jnp.float32) * gates
    partial = result.astype(jnp.bfloat16).reshape(owners, SLAB, width)
    layer_out, normed = reduce_rows(nz, partial, resid, final_gain.reshape(1, width), row_count)
    slots = jnp.concatenate(
        [
            jnp.arange(owners, dtype=jnp.int32) * FINAL,
            request_order // decode_count * FINAL + 1 + request_order % decode_count,
        ]
    )
    chosen = (slots[:, None] == jnp.arange(owners * FINAL, dtype=jnp.int32)).astype(jnp.bfloat16)
    final_normed = jnp.dot(chosen, normed, preferred_element_type=jnp.float32).astype(jnp.bfloat16)
    logits = jnp.dot(final_normed, head_weight, preferred_element_type=jnp.float32)
    return (layer_out, logits)


def on_device(
    prefill_tokens,
    decode_tokens,
    request_order,
    prefill_lengths,
    decode_lengths,
    latent_cache,
    attn_gain,
    w_query,
    w_latent,
    latent_gain,
    key_up,
    value_up,
    w_out,
    ffn_gain,
    expert_ids,
    expert_weights,
    w_gate,
    w_up,
    w_down,
    final_gain,
    head_weight,
):
    owners = lax.axis_size("ep")
    shards = lax.axis_size("vp")
    partial_attn = attend(
        prefill_tokens,
        decode_tokens,
        latent_cache,
        prefill_lengths,
        decode_lengths,
        attn_gain,
        w_query,
        w_latent,
        latent_gain,
        key_up,
        value_up,
        w_out,
    )
    attn = lax.psum(partial_attn, "vp")
    tokens = jnp.concatenate([prefill_tokens, decode_tokens], axis=0)
    resid = (tokens.astype(jnp.float32) + attn).astype(jnp.bfloat16)
    ffn_in = rms_norm(resid.astype(jnp.float32), ffn_gain).astype(jnp.bfloat16)
    row_count = tokens.shape[0]
    model_width = tokens.shape[1]
    share_width = model_width // shards
    capacity = max(2, min(row_count, row_count * TOPK * 2 // owners))
    flat_ids = expert_ids.reshape(-1)
    onehot = (flat_ids[:, None] == jnp.arange(owners, dtype=jnp.int32)[None, :]).astype(jnp.int32)
    earlier = jnp.cumsum(onehot, axis=0) - onehot
    slot_index = jnp.sum(earlier * onehot, axis=1)
    target = flat_ids * capacity + slot_index
    source_rows = jnp.arange(row_count * TOPK, dtype=jnp.int32) // TOPK
    outgoing = (
        jnp.zeros((owners * capacity, model_width), jnp.bfloat16)
        .at[target]
        .set(ffn_in[source_rows])
    )
    outgoing = outgoing.reshape(owners, capacity, model_width)
    arrived = lax.all_to_all(outgoing, "ep", split_axis=0, concat_axis=0, tiled=True)
    item_count = arrived.shape[1]
    flattened = arrived.reshape(owners * item_count, model_width)
    gated = jnp.dot(flattened, w_gate[0], preferred_element_type=jnp.float32)
    upward = jnp.dot(flattened, w_up[0], preferred_element_type=jnp.float32)
    hidden_act = (jax.nn.silu(gated) * upward).astype(jnp.bfloat16)
    result = jnp.dot(hidden_act, w_down[0], preferred_element_type=jnp.float32).reshape(
        owners, item_count, model_width
    )
    summed = lax.psum_scatter(result, "vp", scatter_dimension=2, tiled=True)
    sent_back = lax.all_to_all(summed, "ep", split_axis=0, concat_axis=0, tiled=True)
    picked = sent_back.reshape(owners * capacity, sent_back.shape[2])[target]
    picked = picked.reshape(row_count, TOPK, sent_back.shape[2])
    routed_sum = jnp.sum(expert_weights[:, :, None] * picked, axis=1)
    column = lax.axis_index("vp") * share_width
    resid_share = lax.dynamic_slice_in_dim(resid, column, share_width, 1)
    layer_out = (resid_share.astype(jnp.float32) + routed_sum).astype(jnp.bfloat16)
    prefill_count = prefill_tokens.shape[0]
    decode_count = decode_tokens.shape[0]
    own_rows = layer_out[prefill_count - 1 :]
    everyone = lax.all_gather(own_rows, ("ep", "vp"), axis=0, tiled=True)
    everyone = everyone.reshape(owners, shards, 1 + decode_count, share_width)
    everyone = jnp.transpose(everyone, (0, 2, 1, 3)).reshape(owners, 1 + decode_count, model_width)
    prefill_last = everyone[:, 0]
    decode_rows = everyone[:, 1:].reshape(owners * decode_count, model_width)[request_order]
    final_rows = jnp.concatenate([prefill_last, decode_rows], axis=0)
    final_normed = rms_norm(final_rows.astype(jnp.float32), final_gain).astype(jnp.bfloat16)
    logits = jnp.dot(final_normed, head_weight, preferred_element_type=jnp.float32)
    return (layer_out, logits)


def solution(mesh):
    block = mesh.shape["vp"] == 2 and mesh.shape["ep"] == 16
    return jax.shard_map(
        on_block if block else on_device,
        mesh=mesh,
        in_specs=(
            P("ep", None),
            P("ep", None),
            P(),
            P("ep"),
            P("ep"),
            P("ep", None, None),
            P(),
            P(None, "vp"),
            P(),
            P(),
            P(None, "vp"),
            P(None, "vp"),
            P("vp", None),
            P(),
            P("ep", None),
            P("ep", None),
            P("ep", None, "vp"),
            P("ep", None, "vp"),
            P("ep", "vp", None),
            P(),
            P(None, ("ep", "vp")),
        ),
        out_specs=(P("ep", "vp"), P(None, ("ep", "vp"))),
        check_vma=False,
    )
```

```python
import functools

import jax
import jax.numpy as jnp
from jax import lax
from jax.experimental import pallas as pl
from jax.experimental.pallas import tpu as pltpu
from jax.sharding import PartitionSpec as P

NOPE = 128
ROPE = 64
VD = 128
LAT = 512
TOPK = 6


epsilon = 1e-06
rope_base = 10000.0


def rms_norm(values, gain):
    return values * lax.rsqrt(jnp.mean(values * values, axis=-1, keepdims=True) + epsilon) * gain


def rotate(values, positions):
    half_width = values.shape[-1] // 2
    frequency = rope_base ** (-jnp.arange(half_width, dtype=jnp.float32) * 2.0 / values.shape[-1])
    angles = positions.astype(jnp.float32)[..., None] * frequency
    cosines = jnp.cos(angles)
    sines = jnp.sin(angles)
    lower_half = values[..., :half_width]
    upper_half = values[..., half_width:]
    return jnp.concatenate(
        [lower_half * cosines - upper_half * sines, lower_half * sines + upper_half * cosines],
        axis=-1,
    )


def attend(
    prefill_rows,
    decode_rows,
    cached,
    prefill_len,
    decode_len,
    attn_gain,
    w_query,
    w_latent,
    latent_gain,
    key_up,
    value_up,
    w_out,
):
    tokens = jnp.concatenate([prefill_rows, decode_rows], axis=0)
    prefill_count = prefill_rows.shape[0]
    row_count = tokens.shape[0]
    head_count = w_query.shape[1] // (NOPE + ROPE)
    positions = jnp.concatenate(
        [prefill_len[0] + jnp.arange(prefill_count, dtype=jnp.int32), decode_len]
    )
    normed = rms_norm(tokens.astype(jnp.float32), attn_gain).astype(jnp.bfloat16)
    queries = jnp.dot(normed, w_query, preferred_element_type=jnp.float32).reshape(
        row_count, head_count, NOPE + ROPE
    )
    query_nope = queries[..., :NOPE].astype(jnp.bfloat16)
    query_rope = rotate(queries[..., NOPE:], positions[:, None]).astype(jnp.bfloat16)
    latent = jnp.dot(normed, w_latent, preferred_element_type=jnp.float32)
    latent_normed = rms_norm(latent[:, :LAT], latent_gain)
    new_keys = jnp.concatenate([latent_normed, rotate(latent[:, LAT:], positions)], axis=1).astype(
        jnp.bfloat16
    )
    key_heads = key_up.reshape(LAT, head_count, NOPE)
    absorbed = jnp.einsum(
        "rhn,lhn->rhl", query_nope, key_heads, preferred_element_type=jnp.float32
    ).astype(jnp.bfloat16)
    query_all = jnp.concatenate([absorbed, query_rope], axis=-1)
    factor = 1.0 / jnp.sqrt(jnp.float32(NOPE + ROPE))
    cache_len = cached.shape[1]
    prefill_keys = jnp.concatenate([cached[0], new_keys[:prefill_count]], axis=0)
    scores = (
        jnp.einsum(
            "chk,jk->chj",
            query_all[:prefill_count],
            prefill_keys,
            preferred_element_type=jnp.float32,
        )
        * factor
    )
    key_index = jnp.arange(cache_len + prefill_count, dtype=jnp.int32)
    row_index = jnp.arange(prefill_count, dtype=jnp.int32)
    visible = jnp.where(
        key_index[None, :] < cache_len,
        key_index[None, :] < prefill_len[0],
        key_index[None, :] - cache_len <= row_index[:, None],
    )
    expo = jnp.exp(jnp.where(visible[:, None, :], scores, -jnp.inf))
    attn_probs = (expo / jnp.sum(expo, axis=-1, keepdims=True)).astype(jnp.bfloat16)
    prefill_context = jnp.einsum(
        "chj,jl->chl", attn_probs, prefill_keys[:, :LAT], preferred_element_type=jnp.float32
    ).astype(jnp.bfloat16)
    decode_query = query_all[prefill_count:]
    decode_cache = cached[1:]
    own_keys = new_keys[prefill_count:]
    cache_scores = (
        jnp.einsum("dhk,dsk->dhs", decode_query, decode_cache, preferred_element_type=jnp.float32)
        * factor
    )
    self_scores = (
        jnp.einsum("dhk,dk->dh", decode_query, own_keys, preferred_element_type=jnp.float32)
        * factor
    )
    cache_visible = jnp.arange(cache_len, dtype=jnp.int32)[None, :] < decode_len[:, None]
    cache_expo = jnp.exp(jnp.where(cache_visible[:, None, :], cache_scores, -jnp.inf))
    self_expo = jnp.exp(self_scores)
    totals = jnp.sum(cache_expo, axis=-1) + self_expo
    cache_probs = (cache_expo / totals[..., None]).astype(jnp.bfloat16)
    self_probs = (self_expo / totals).astype(jnp.bfloat16)
    decode_context = jnp.einsum(
        "dhs,dsl->dhl", cache_probs, decode_cache[..., :LAT], preferred_element_type=jnp.float32
    )
    decode_context = (
        decode_context
        + self_probs.astype(jnp.float32)[..., None] * own_keys[:, None, :LAT].astype(jnp.float32)
    ).astype(jnp.bfloat16)
    context = jnp.concatenate([prefill_context, decode_context], axis=0)
    value_heads = value_up.reshape(LAT, head_count, VD)
    head_out = jnp.einsum(
        "rhl,lhv->rhv", context, value_heads, preferred_element_type=jnp.float32
    ).astype(jnp.bfloat16)
    return jnp.dot(
        head_out.reshape(row_count, head_count * VD), w_out, preferred_element_type=jnp.float32
    )


MESH = pl.DeviceIdType.MESH
SLAB = 80
CODE_ROW = 72
LANES = 128
FINAL = 8


def place():
    e = lax.axis_index("ep")
    return e // 4, (e // 2) % 2, e % 2, lax.axis_index("vp")


def at(z, x, c, y):
    return {"ep": z * 4 + x * 2 + c, "vp": y}


def remote(src, dst, send, recv, target):
    return pltpu.make_async_remote_copy(
        src_ref=src, dst_ref=dst, send_sem=send, recv_sem=recv, device_id=target, device_id_type=MESH
    )


def gather_kernel(nz, part_ref, tok_ref, gain_ref, code_ref, resid_ref, all_ref, got, ys, yr, us, ur, ds, dr, xs, xr, cs, cr, ws, wr, bs, br):
    z, x, c, y = place()
    barrier = pltpu.get_barrier_semaphore()
    for target in (at(z, x, c, 1 - y), at(z, 1 - x, c, y), at(z, x, 1 - c, y)):
        pl.semaphore_signal(barrier, inc=1, device_id=target, device_id_type=MESH)

    for k in range(1, nz):
        pl.semaphore_signal(barrier, inc=1, device_id=at((z + k) % nz, x, c, y), device_id_type=MESH)
    pl.semaphore_wait(barrier, nz + 2)

    swap = remote(part_ref, got, ys, yr, at(z, x, c, 1 - y))
    swap.start()
    swap.wait()
    mine = z * 4 + x * 2 + c
    attn = part_ref[...].astype(jnp.float32) + got[...].astype(jnp.float32)
    resid = (tok_ref[...].astype(jnp.float32) + attn).astype(jnp.bfloat16)
    resid_ref[...] = resid
    ffn_in = rms_norm(resid.astype(jnp.float32), gain_ref[...])
    all_ref[mine] = (ffn_in + code_ref[...].astype(jnp.float32)).astype(jnp.bfloat16)

    width = tok_ref.shape[1]
    band = width * 5 // 16 // LANES * LANES
    main = width - band

    def slab(zo, xo, co):
        return all_ref.at[zo * 4 + xo * 2 + co, :, pl.ds(pl.multiple_of(y * band, LANES), main)]

    def strip(zo, xo, co, yo):
        return all_ref.at[zo * 4 + xo * 2 + co, :, pl.ds(pl.multiple_of(yo * main, LANES), band)]

    def lend(zo, xo):
        s = strip(zo, xo, c, y)
        return remote(s, s, ws.at[xo, zo], wr.at[xo, zo], at(z, x, c, 1 - y))

    def lend_in(zo, xo):
        s = strip(zo, xo, c, 1 - y)
        return remote(s, s, ws.at[xo, zo], wr.at[xo, zo], at(z, x, c, 1 - y))

    def rest(zo, xo):
        s = strip(zo, xo, c, 1 - y)
        return remote(s, s, bs.at[xo, zo], br.at[xo, zo], at(z, x, 1 - c, y))

    def rest_in(zo, xo):
        s = strip(zo, xo, 1 - c, 1 - y)
        return remote(s, s, bs.at[xo, zo], br.at[xo, zo], at(z, x, 1 - c, y))

    others = [((z + k) % nz, (x + dx) % 2) for k in range(nz) for dx in range(2) if k + dx > 0]

    def up(step):
        s = slab(z - step, x, c)
        return remote(s, s, us.at[step], ur.at[step], at(z + 1, x, c, y))

    def up_in(step):
        s = slab(z - 1 - step, x, c)
        return remote(s, s, us.at[step], ur.at[step], at(z - 1, x, c, y))

    def down(step):
        s = slab(z + step, x, c)
        return remote(s, s, ds.at[step], dr.at[step], at(z - 1, x, c, y))

    def down_in(step):
        s = slab(z + 1 + step, x, c)
        return remote(s, s, ds.at[step], dr.at[step], at(z + 1, x, c, y))

    def across(zo):
        s = slab(zo, x, c)
        return remote(s, s, xs.at[zo], xr.at[zo], at(z, 1 - x, c, y))

    def across_in(zo):
        s = slab(zo, 1 - x, c)
        return remote(s, s, xs.at[zo], xr.at[zo], at(z, 1 - x, c, y))

    def over(zo, xo):
        s = slab(zo, xo, c)
        return remote(s, s, cs.at[xo, zo], cr.at[xo, zo], at(z, x, 1 - c, y))

    def over_in(zo, xo):
        s = slab(zo, xo, 1 - c)
        return remote(s, s, cs.at[xo, zo], cr.at[xo, zo], at(z, x, 1 - c, y))

    def when(cond, fun):
        pl.when(cond)(fun)

    when(z + 1 < nz, lambda: up(0).start())
    when(z > 0, lambda: down(0).start())
    across(z).start()
    over(z, x).start()
    rest(z, x).start()
    for step in range(nz - 1):

        @pl.when(z - 1 - step >= 0)
        def _():
            up_in(step).wait_recv()
            if step + 1 < nz - 1:
                when(z + 1 < nz, lambda: up(step + 1).start())
            across(z - 1 - step).start()
            lend(z - 1 - step, x).start()
            over(z - 1 - step, x).start()

        @pl.when(z + 1 + step < nz)
        def _():
            down_in(step).wait_recv()
            if step + 1 < nz - 1:
                when(z > 0, lambda: down(step + 1).start())
            across(z + 1 + step).start()
            lend(z + 1 + step, x).start()
            over(z + 1 + step, x).start()

    def land(zo):
        across_in(zo).wait_recv()
        lend(zo, 1 - x).start()
        over(zo, 1 - x).start()

    land(z)
    for step in range(nz - 1):
        when(z - 1 - step >= 0, lambda: land(z - 1 - step))
        when(z + 1 + step < nz, lambda: land(z + 1 + step))
    for zo, xo in others:
        lend_in(zo, xo).wait_recv()
        rest(zo, xo).start()
    for zo in range(nz):
        for xo in range(2):
            over_in(zo, xo).wait_recv()
            rest_in(zo, xo).wait_recv()
    for zo, xo in others:
        lend(zo, xo).wait_send()
    for zo in range(nz):
        across(zo).wait_send()
        for xo in range(2):
            over(zo, xo).wait_send()
            rest(zo, xo).wait_send()
    for step in range(nz - 1):
        when((z + 1 < nz) & (z - step >= 0), lambda: up(step).wait_send())
        when((z > 0) & (z + step < nz), lambda: down(step).wait_send())


def gather(nz, partial, tokens, gain, code):
    rows, width = tokens.shape
    dma = pltpu.SemaphoreType.DMA
    return pl.pallas_call(
        functools.partial(gather_kernel, nz),
        name="gather_tokens",
        out_shape=(
            jax.ShapeDtypeStruct((rows, width), jnp.bfloat16),
            jax.ShapeDtypeStruct((nz * 4, rows, width), jnp.bfloat16),
        ),
        in_specs=[pl.BlockSpec(memory_space=pltpu.VMEM)] * 4,
        out_specs=(pl.BlockSpec(memory_space=pltpu.VMEM),) * 2,
        scratch_shapes=[
            pltpu.VMEM((rows, width), jnp.bfloat16),
            dma,
            dma,
            dma((nz - 1,)),
            dma((nz - 1,)),
            dma((nz - 1,)),
            dma((nz - 1,)),
            dma((nz,)),
            dma((nz,)),
            dma((2, nz)),
            dma((2, nz)),
            dma((2, nz)),
            dma((2, nz)),
            dma((2, nz)),
            dma((2, nz)),
        ],
        compiler_params=pltpu.CompilerParams(
            collective_id=0, has_side_effects=True, vmem_limit_bytes=40 * 1024 * 1024
        ),
    )(partial, tokens, gain, code)


def reduce_kernel(nz, p_ref, resid_ref, gain_ref, out_ref, normed_ref, fin_ref, cin, s1, ya, xb, xa, yb, s2a, s2b, s3, zin, fbuf, c_s, c_r, ya_s, ya_r, xb_s, xb_r, xa_s, xa_r, yb_s, yb_r, z_s, z_r, f_s, f_r, g_s, g_r):
    z, x, c, y = place()
    share = s3.shape[-1]
    half = share // 2
    barrier = pltpu.get_barrier_semaphore()
    plane = [(dx, dc, dy) for dx in range(2) for dc in range(2) for dy in range(2) if (dx, dc, dy) != (0, 0, 0)]

    def beside(k):
        dx, dc, dy = plane[k]
        return at(z, (x + dx) % 2, (c + dc) % 2, (y + dy) % 2)

    def along(k):
        return at((z + k) % nz, x, c, y)

    for k in range(len(plane)):
        pl.semaphore_signal(barrier, inc=1, device_id=beside(k), device_id_type=MESH)
    for k in range(1, nz):
        pl.semaphore_signal(barrier, inc=1, device_id=along(k), device_id_type=MESH)
    pl.semaphore_wait(barrier, len(plane) + nz - 1)

    def add(a, b):
        return (a.astype(jnp.float32) + b.astype(jnp.float32)).astype(jnp.bfloat16)

    def cols(yo, part):
        return pl.ds(pl.multiple_of(yo * share + part * half, LANES), half)

    def core_copy(zo, xo):
        return remote(
            p_ref.at[zo * 4 + xo * 2 + 1 - c], cin.at[zo * 2 + xo], c_s.at[zo, xo], c_r.at[zo, xo], at(z, x, 1 - c, y)
        )

    def ya_copy(zo, xo):
        return remote(
            s1.at[zo * 2 + xo, :, cols(1 - y, 0)], ya.at[zo * 2 + xo], ya_s.at[zo, xo], ya_r.at[zo, xo], at(z, x, c, 1 - y)
        )

    def xb_copy(zo, yo):
        return remote(
            s1.at[zo * 2 + 1 - x, :, cols(yo, 1)], xb.at[zo * 2 + yo], xb_s.at[zo, yo], xb_r.at[zo, yo], at(z, 1 - x, c, y)
        )

    def xa_copy(zo):
        return remote(s2a.at[zo * 2 + 1 - x], xa.at[zo], xa_s.at[zo], xa_r.at[zo], at(z, 1 - x, c, y))

    def yb_copy(zo):
        return remote(s2b.at[zo * 2 + 1 - y], yb.at[zo], yb_s.at[zo], yb_r.at[zo], at(z, x, c, 1 - y))

    def z_copy(k):
        return remote(s3.at[(z + k) % nz], zin.at[k - 1], z_s.at[k - 1], z_r.at[k - 1], along(k))

    order = [(z + 1 + i) % nz for i in range(nz)]
    for zo in order:
        for xo in range(2):
            core_copy(zo, xo).start()
    for zo in order:
        for xo in range(2):
            core_copy(zo, xo).wait_recv()
            s1[zo * 2 + xo] = add(p_ref[zo * 4 + xo * 2 + c], cin[zo * 2 + xo])
            ya_copy(zo, xo).start()
        for yo in range(2):
            xb_copy(zo, yo).start()
    for zo in order:
        for side in range(2):
            ya_copy(zo, side).wait_recv()
            s2a[zo * 2 + side] = add(s1[zo * 2 + side, :, cols(y, 0)], ya[zo * 2 + side])
            xb_copy(zo, side).wait_recv()
            s2b[zo * 2 + side] = add(s1[zo * 2 + x, :, cols(side, 1)], xb[zo * 2 + side])
        xa_copy(zo).start()
        yb_copy(zo).start()
    for i, zo in enumerate(order):
        xa_copy(zo).wait_recv()
        yb_copy(zo).wait_recv()
        s3[zo, :, :half] = add(s2a[zo * 2 + x], xa[zo])
        s3[zo, :, half:] = add(s2b[zo * 2 + y], yb[zo])
        if i < nz - 1:
            z_copy(i + 1).start()
    total = s3[z].astype(jnp.float32)
    for k in range(1, nz):
        z_copy(k).wait_recv()
        total = total + zin[k - 1].astype(jnp.float32)
    own = resid_ref[:, pl.ds(pl.multiple_of(y * share, LANES), share)].astype(jnp.float32)
    fbuf[...] = own + total
    out_ref[...] = fbuf[: out_ref.shape[0], :].astype(jnp.bfloat16)

    def piece(zo, xo, co, yo):
        return fin_ref.at[zo * 4 + xo * 2 + co, :, pl.ds(pl.multiple_of(yo * share, LANES), share)]

    mine = z * 4 + x * 2 + c
    fin_ref[mine, :, pl.ds(pl.multiple_of(y * share, LANES), share)] = fbuf[63:71, :].astype(jnp.bfloat16)

    def f_copy(k):
        b = piece(z, x, c, y)
        return remote(b, b, f_s.at[k - 1], f_r.at[k - 1], along(k))

    def g_copy(k, d):
        b = piece((z + d) % nz, x, c, y)
        return remote(b, b, g_s.at[k, d], g_r.at[k, d], beside(k))

    def g_in(k, d):
        dx, dc, dy = plane[k]
        b = piece((z + d) % nz, (x + dx) % 2, (c + dc) % 2, (y + dy) % 2)
        return remote(b, b, g_s.at[k, d], g_r.at[k, d], beside(k))

    def f_in(k):
        b = piece((z + nz - k) % nz, x, c, y)
        return remote(b, b, f_s.at[k - 1], f_r.at[k - 1], along(k))

    for k in range(1, nz):
        f_copy(k).start()
    for k in range(len(plane)):
        g_copy(k, 0).start()
    for d in range(1, nz):
        f_in(d).wait_recv()
        for k in range(len(plane)):
            g_copy(k, nz - d).start()
    for k in range(len(plane)):
        for d in range(nz):
            g_in(k, d).wait_recv()
    rows = rms_norm(fin_ref[...].astype(jnp.float32), gain_ref[...])
    normed_ref[...] = rows.reshape(normed_ref.shape).astype(jnp.bfloat16)
    for k in range(len(plane)):
        for d in range(nz):
            g_copy(k, d).wait_send()
    for k in range(1, nz):
        f_copy(k).wait_send()
        z_copy(k).wait_send()
    for zo in range(nz):
        xa_copy(zo).wait_send()
        yb_copy(zo).wait_send()
        for side in range(2):
            core_copy(zo, side).wait_send()
            ya_copy(zo, side).wait_send()
            xb_copy(zo, side).wait_send()


def reduce_rows(nz, partial, resid, gain, row_count):
    owners, rows, width = partial.shape
    share = width // 2
    half = share // 2
    dma = pltpu.SemaphoreType.DMA
    buf = lambda *shape: pltpu.VMEM(shape, jnp.bfloat16)
    return pl.pallas_call(
        functools.partial(reduce_kernel, nz),
        name="reduce_rows",
        out_shape=(
            jax.ShapeDtypeStruct((row_count, share), jnp.bfloat16),
            jax.ShapeDtypeStruct((owners * FINAL, width), jnp.bfloat16),
        ),
        in_specs=[pl.BlockSpec(memory_space=pltpu.VMEM)] * 3,
        out_specs=(pl.BlockSpec(memory_space=pltpu.VMEM),) * 2,
        scratch_shapes=[
            buf(owners, FINAL, width),
            buf(nz * 2, rows, width),
            buf(nz * 2, rows, width),
            buf(nz * 2, rows, half),
            buf(nz * 2, rows, half),
            buf(nz, rows, half),
            buf(nz, rows, half),
            buf(nz * 2, rows, half),
            buf(nz * 2, rows, half),
            buf(nz, rows, share),
            buf(nz - 1, rows, share),
            pltpu.VMEM((rows, share), jnp.float32),
        ]
        + [dma((nz, 2))] * 6
        + [dma((nz,))] * 4
        + [dma((nz - 1,))] * 4
        + [dma((7, nz))] * 2,
        compiler_params=pltpu.CompilerParams(
            collective_id=1, has_side_effects=True, vmem_limit_bytes=48 * 1024 * 1024
        ),
    )(partial, resid, gain)


def attention_kernel(heads, pf, rows_of, tok_ref, gain_ref, cos_ref, sin_ref, len_ref, lgain_ref, wq_hbm, wl_hbm, cache_hbm, ku_hbm, vu_hbm, wo_hbm, out_ref, wq, wl, cache, ku, vu, wo, sems):
    pairs = [(wq_hbm, wq), (wl_hbm, wl), (cache_hbm, cache), (ku_hbm, ku), (vu_hbm, vu), (wo_hbm, wo)]
    loads = [pltpu.make_async_copy(a, b, sems.at[i]) for i, (a, b) in enumerate(pairs)]
    for load in loads:
        load.start()
    rows = tok_ref.shape[0]
    f32, bf16 = jnp.float32, jnp.bfloat16
    dot = functools.partial(jnp.dot, preferred_element_type=f32)
    nt = lambda a, b: lax.dot_general(a, b, (((1,), (1,)), ((), ())), preferred_element_type=f32)
    normed = rms_norm(tok_ref[...].astype(f32), gain_ref[...]).astype(bf16)
    cosines, sines = cos_ref[...], sin_ref[...]

    def turn(v):
        half = ROPE // 2
        return v * cosines + jnp.concatenate([v[:, half:], v[:, :half]], axis=1) * sines

    loads[0].wait()
    queries = dot(normed, wq[...])
    loads[1].wait()
    latent = nt(normed, wl[...])
    key_lat = rms_norm(latent[:, :LAT], lgain_ref[...]).astype(bf16)
    key_rope = turn(latent[:, LAT:]).astype(bf16)
    loads[2].wait()
    entries, cache_len = cache.shape[0], cache.shape[2]
    old_lat = [cache[e, :LAT, :] for e in range(entries)]
    old_rope = [cache[e, LAT:, :] for e in range(entries)]
    row = lax.broadcasted_iota(jnp.int32, (rows, 1), 0)
    entry = jnp.where(row < pf, 0, jnp.where(row < rows_of, row - pf + 1, entries))
    start = entry * cache_len
    key = lax.broadcasted_iota(jnp.int32, (rows, entries * cache_len), 1)
    old_seen = (key >= start) & (key < start + len_ref[...])
    col = lax.broadcasted_iota(jnp.int32, (rows, rows), 1)
    new_seen = (col == row) | ((row < pf) & (col <= row))
    factor = 1.0 / jnp.sqrt(jnp.float32(NOPE + ROPE))
    loads[3].wait()
    outs = []
    for h in range(heads):
        base = h * (NOPE + ROPE)
        q_nope = queries[:, base : base + NOPE].astype(bf16)
        q_rope = turn(queries[:, base + NOPE : base + NOPE + ROPE]).astype(bf16)
        absorbed = nt(q_nope, ku[:, h * NOPE : (h + 1) * NOPE]).astype(bf16)
        old = [dot(absorbed, old_lat[e]) + dot(q_rope, old_rope[e]) for e in range(entries)]
        old = jnp.concatenate(old, axis=1) * factor
        new = (nt(absorbed, key_lat) + nt(q_rope, key_rope)) * factor
        old = jnp.exp(jnp.where(old_seen, old, -jnp.inf))
        new = jnp.exp(jnp.where(new_seen, new, -jnp.inf))
        total = jnp.sum(old, axis=1, keepdims=True) + jnp.sum(new, axis=1, keepdims=True)
        old = (old / total).astype(bf16)
        new = (new / total).astype(bf16)
        context = dot(new, key_lat)
        for e in range(entries):
            context = context + nt(old[:, e * cache_len : (e + 1) * cache_len], old_lat[e])
        context = context.astype(bf16)
        if h == 0:
            loads[4].wait()
        outs.append(dot(context, vu[:, h * VD : (h + 1) * VD]).astype(bf16))
    loads[5].wait()
    out_ref[...] = dot(jnp.concatenate(outs, axis=1), wo[...]).astype(bf16)


def attention(tokens, pf, nd, prefill_len, decode_len, cached, attn_gain, w_query, w_latent, latent_gain, key_up, value_up, w_out):
    rows, width = tokens.shape
    spare = rows - pf - nd
    steps = jnp.arange(pf, dtype=jnp.int32)
    none = jnp.zeros((spare,), jnp.int32)
    positions = jnp.concatenate([prefill_len[0] + steps, decode_len, none])
    lengths = jnp.concatenate([prefill_len[0] + 0 * steps, decode_len, none])[:, None]
    half = ROPE // 2
    frequency = rope_base ** (-jnp.arange(half, dtype=jnp.float32) * 2.0 / ROPE)
    angles = positions.astype(jnp.float32)[:, None] * frequency
    cosines, sines = jnp.cos(angles), jnp.sin(angles)
    vmem = pl.BlockSpec(memory_space=pltpu.VMEM)
    hbm = pl.BlockSpec(memory_space=pltpu.HBM)
    large = (w_query, w_latent.T, jnp.swapaxes(cached, 1, 2), key_up, value_up, w_out)
    return pl.pallas_call(
        functools.partial(attention_kernel, w_query.shape[1] // (NOPE + ROPE), pf, pf + nd),
        name="attention",
        out_shape=jax.ShapeDtypeStruct((rows, width), jnp.bfloat16),
        in_specs=[vmem] * 6 + [hbm] * 6,
        out_specs=vmem,
        scratch_shapes=[pltpu.VMEM(a.shape, a.dtype) for a in large] + [pltpu.SemaphoreType.DMA((6,))],
        compiler_params=pltpu.CompilerParams(vmem_limit_bytes=60 * 1024 * 1024),
    )(
        tokens,
        attn_gain.reshape(1, width),
        jnp.concatenate([cosines, cosines], axis=1),
        jnp.concatenate([-sines, sines], axis=1),
        lengths,
        latent_gain.reshape(1, LAT),
        *large,
    )


def gate_code(expert_ids, expert_weights, owners, width):
    named = expert_ids[:, :, None] == jnp.arange(owners, dtype=jnp.int32)
    dense = jnp.sum(jnp.where(named, expert_weights[:, :, None], 0.0), axis=1)
    flat = jnp.pad(dense.T, ((0, 0), (0, LANES - dense.shape[0]))).reshape(1, width)
    high = lax.reduce_precision(flat, 8, 7)
    middle = lax.reduce_precision(flat - high, 8, 7)
    low = flat - high - middle
    code = jnp.concatenate([high, middle, low], axis=0).astype(jnp.bfloat16)
    return jnp.pad(code, ((CODE_ROW, SLAB - CODE_ROW - 3), (0, 0)))


def on_block(
    prefill_tokens,
    decode_tokens,
    request_order,
    prefill_lengths,
    decode_lengths,
    latent_cache,
    attn_gain,
    w_query,
    w_latent,
    latent_gain,
    key_up,
    value_up,
    w_out,
    ffn_gain,
    expert_ids,
    expert_weights,
    w_gate,
    w_up,
    w_down,
    final_gain,
    head_weight,
):
    owners = lax.axis_size("ep")
    nz = owners // 4
    tokens = jnp.concatenate([prefill_tokens, decode_tokens], axis=0)
    row_count, width = tokens.shape
    prefill_count, decode_count = prefill_tokens.shape[0], decode_tokens.shape[0]
    tokens = jnp.pad(tokens, ((0, SLAB - row_count), (0, 0)))
    partial_attn = attention(
        tokens,
        prefill_count,
        decode_count,
        prefill_lengths,
        decode_lengths,
        latent_cache,
        attn_gain,
        w_query,
        w_latent,
        latent_gain,
        key_up,
        value_up,
        w_out,
    )
    resid, arrived = gather(
        nz,
        partial_attn,
        tokens,
        ffn_gain.reshape(1, width),
        gate_code(expert_ids, expert_weights, owners, width),
    )
    me = lax.axis_index("ep")
    codes = lax.dynamic_slice(arrived, (0, CODE_ROW, me * LANES), (owners, 3, LANES))
    gates = jnp.sum(codes.astype(jnp.float32), axis=1)[:, :SLAB].reshape(owners * SLAB, 1)
    flattened = arrived.reshape(owners * SLAB, width)
    gated = jnp.dot(flattened, w_gate[0], preferred_element_type=jnp.float32)
    upward = jnp.dot(flattened, w_up[0], preferred_element_type=jnp.float32)
    hidden_act = (jax.nn.silu(gated) * upward).astype(jnp.bfloat16)
    result = jnp.dot(hidden_act, w_down[0], preferred_element_type=jnp.float32) * gates
    partial = result.astype(jnp.bfloat16).reshape(owners, SLAB, width)
    layer_out, normed = reduce_rows(nz, partial, resid, final_gain.reshape(1, width), row_count)
    slots = jnp.concatenate(
        [
            jnp.arange(owners, dtype=jnp.int32) * FINAL,
            request_order // decode_count * FINAL + 1 + request_order % decode_count,
        ]
    )
    chosen = (slots[:, None] == jnp.arange(owners * FINAL, dtype=jnp.int32)).astype(jnp.bfloat16)
    final_normed = jnp.dot(chosen, normed, preferred_element_type=jnp.float32).astype(jnp.bfloat16)
    logits = jnp.dot(final_normed, head_weight, preferred_element_type=jnp.float32)
    return (layer_out, logits)


def on_device(
    prefill_tokens,
    decode_tokens,
    request_order,
    prefill_lengths,
    decode_lengths,
    latent_cache,
    attn_gain,
    w_query,
    w_latent,
    latent_gain,
    key_up,
    value_up,
    w_out,
    ffn_gain,
    expert_ids,
    expert_weights,
    w_gate,
    w_up,
    w_down,
    final_gain,
    head_weight,
):
    owners = lax.axis_size("ep")
    shards = lax.axis_size("vp")
    partial_attn = attend(
        prefill_tokens,
        decode_tokens,
        latent_cache,
        prefill_lengths,
        decode_lengths,
        attn_gain,
        w_query,
        w_latent,
        latent_gain,
        key_up,
        value_up,
        w_out,
    )
    attn = lax.psum(partial_attn, "vp")
    tokens = jnp.concatenate([prefill_tokens, decode_tokens], axis=0)
    resid = (tokens.astype(jnp.float32) + attn).astype(jnp.bfloat16)
    ffn_in = rms_norm(resid.astype(jnp.float32), ffn_gain).astype(jnp.bfloat16)
    row_count = tokens.shape[0]
    model_width = tokens.shape[1]
    share_width = model_width // shards
    capacity = max(2, min(row_count, row_count * TOPK * 2 // owners))
    flat_ids = expert_ids.reshape(-1)
    onehot = (flat_ids[:, None] == jnp.arange(owners, dtype=jnp.int32)[None, :]).astype(jnp.int32)
    earlier = jnp.cumsum(onehot, axis=0) - onehot
    slot_index = jnp.sum(earlier * onehot, axis=1)
    target = flat_ids * capacity + slot_index
    source_rows = jnp.arange(row_count * TOPK, dtype=jnp.int32) // TOPK
    outgoing = (
        jnp.zeros((owners * capacity, model_width), jnp.bfloat16)
        .at[target]
        .set(ffn_in[source_rows])
    )
    outgoing = outgoing.reshape(owners, capacity, model_width)
    arrived = lax.all_to_all(outgoing, "ep", split_axis=0, concat_axis=0, tiled=True)
    item_count = arrived.shape[1]
    flattened = arrived.reshape(owners * item_count, model_width)
    gated = jnp.dot(flattened, w_gate[0], preferred_element_type=jnp.float32)
    upward = jnp.dot(flattened, w_up[0], preferred_element_type=jnp.float32)
    hidden_act = (jax.nn.silu(gated) * upward).astype(jnp.bfloat16)
    result = jnp.dot(hidden_act, w_down[0], preferred_element_type=jnp.float32).reshape(
        owners, item_count, model_width
    )
    summed = lax.psum_scatter(result, "vp", scatter_dimension=2, tiled=True)
    sent_back = lax.all_to_all(summed, "ep", split_axis=0, concat_axis=0, tiled=True)
    picked = sent_back.reshape(owners * capacity, sent_back.shape[2])[target]
    picked = picked.reshape(row_count, TOPK, sent_back.shape[2])
    routed_sum = jnp.sum(expert_weights[:, :, None] * picked, axis=1)
    column = lax.axis_index("vp") * share_width
    resid_share = lax.dynamic_slice_in_dim(resid, column, share_width, 1)
    layer_out = (resid_share.astype(jnp.float32) + routed_sum).astype(jnp.bfloat16)
    prefill_count = prefill_tokens.shape[0]
    decode_count = decode_tokens.shape[0]
    own_rows = layer_out[prefill_count - 1 :]
    everyone = lax.all_gather(own_rows, ("ep", "vp"), axis=0, tiled=True)
    everyone = everyone.reshape(owners, shards, 1 + decode_count, share_width)
    everyone = jnp.transpose(everyone, (0, 2, 1, 3)).reshape(owners, 1 + decode_count, model_width)
    prefill_last = everyone[:, 0]
    decode_rows = everyone[:, 1:].reshape(owners * decode_count, model_width)[request_order]
    final_rows = jnp.concatenate([prefill_last, decode_rows], axis=0)
    final_normed = rms_norm(final_rows.astype(jnp.float32), final_gain).astype(jnp.bfloat16)
    logits = jnp.dot(final_normed, head_weight, preferred_element_type=jnp.float32)
    return (layer_out, logits)


def solution(mesh):
    block = mesh.shape["vp"] == 2 and mesh.shape["ep"] == 16
    return jax.shard_map(
        on_block if block else on_device,
        mesh=mesh,
        in_specs=(
            P("ep", None),
            P("ep", None),
            P(),
            P("ep"),
            P("ep"),
            P("ep", None, None),
            P(),
            P(None, "vp"),
            P(),
            P(),
            P(None, "vp"),
            P(None, "vp"),
            P("vp", None),
            P(),
            P("ep", None),
            P("ep", None),
            P("ep", None, "vp"),
            P("ep", None, "vp"),
            P("ep", "vp", None),
            P(),
            P(None, ("ep", "vp")),
        ),
        out_specs=(P("ep", "vp"), P(None, ("ep", "vp"))),
        check_vma=False,
    )
```
